1024 devices in a mesh: zero: 8 (over x, core), expert: 128 (over y, z).
Axes of the slice: x: 4, y: 8, z: 16, core: 2. Of those that a mesh axis runs over, the one named last changes fastest.
Arguments:
- mom_values: bfloat16 [512, 512, 2048], P('expert', 'zero'), may hold values from -1 to 1
- mom_scale: float32 [512, 512], P('expert', 'zero'), may hold values from 0.5 to 2
- gradients: bfloat16 [512, 512, 2048], P('expert', 'zero'), may hold values from -32400 to 32400
Outputs:
- update: bfloat16 [512, 512, 2048], P('expert', 'zero')
The draws below stay inside these ranges and needn't reach their ends.
All inputs are finite; a program needn't handle non-finite values.
Results may differ from the reference program's by a relative error of at most 0.0061.
Values may be sent and summed in bfloat16 or wider, within the bound.
A program may use at most 32 MiB of HBM per device.

```python
import math
import jax
import jax.numpy as jnp
from jax import lax

MODEL_D = 2048
EXPERT_FF = 512
ITERS = 2
MATS = 512


def draw_gradients(key, part):
    key_noise, key_rows, key_cols = jax.random.split(key, 3)
    full_shape = (MATS, EXPERT_FF, MODEL_D)
    matrix_pos = jnp.arange(MATS, dtype=jnp.float32) / max(MATS - 1, 1)
    row_pos = jnp.arange(EXPERT_FF, dtype=jnp.float32) / max(EXPERT_FF - 1, 1)
    rising = 3.0 ** (matrix_pos[:, None, None] + row_pos[None, :, None])
    row_scales = jnp.exp(jax.random.uniform(key_rows, (MATS, EXPERT_FF, 1), dtype=jnp.float32) * math.log(10.0))
    column_scales = jnp.exp(jax.random.uniform(key_cols, (MATS, 1, MODEL_D), dtype=jnp.float32) * math.log(10.0))
    noise = jax.random.truncated_normal(key_noise, -4.0, 4.0, full_shape, dtype=jnp.float32)
    return (noise * row_scales * column_scales * rising).astype(jnp.bfloat16)


def levels(stream_key, extent, cuts, least, high):
    level, own = 1.0, jax.random.fold_in(stream_key, 6)
    for position, parts in cuts:
        heights = jnp.exp(jax.random.uniform(jax.random.fold_in(own, position), (parts,), jnp.float32, least / len(cuts), high / len(cuts)))
        level = level * jnp.repeat(heights, extent[position] // parts).reshape([-1 if axis == position else 1 for axis in range(len(extent))])
    return level


def setup_inputs(seed: int = 0) -> dict:
    streams_of = jax.random.split(jax.random.key(seed), 4)
    return {
        "mom_values": jnp.clip(jax.random.uniform(streams_of[0], (MATS, EXPERT_FF, MODEL_D), jnp.float32, -1.0, 1.0) * levels(streams_of[0], (MATS, EXPERT_FF, MODEL_D), ((0, 128), (1, 8)), -0.4, 0.0), -1.0, 1.0).astype(jnp.bfloat16),
        "mom_scale": jnp.clip(jnp.exp(math.log(2.0) - 1.3862944 * jax.random.uniform(streams_of[1], (MATS, EXPERT_FF), jnp.float32) ** levels(streams_of[1], (MATS, EXPERT_FF), ((0, 128), (1, 8)), -0.2, 0.2)), 0.5, 2.0),
        "gradients": draw_gradients(jax.random.fold_in(streams_of[3], 71), 0),
    }


coeff_linear = 3.4445
coeff_cubic = -4.775
coeff_quintic = 2.0315
decay_rate = 0.95
clip_level = 1.0
epsilon = 1e-06

def newton_chain(gram_matrix, squared_norm):
    identity = jnp.eye(gram_matrix.shape[0], dtype=jnp.float32)
    gnorm = (gram_matrix / (squared_norm + epsilon)).astype(jnp.bfloat16)
    square = jnp.dot(gnorm, gnorm, preferred_element_type=jnp.float32)
    polynomial = (coeff_linear * identity + coeff_cubic * gnorm.astype(jnp.float32) + coeff_quintic * square).astype(jnp.bfloat16)
    for sweep in range(ITERS - 1):
        halfway = jnp.dot(polynomial, gnorm, preferred_element_type=jnp.float32).astype(jnp.bfloat16)
        conjugated = jnp.dot(halfway, polynomial.T, preferred_element_type=jnp.float32).astype(jnp.bfloat16)
        square = jnp.dot(conjugated, conjugated, preferred_element_type=jnp.float32)
        quintic = (coeff_cubic * conjugated.astype(jnp.float32) + coeff_quintic * square).astype(jnp.bfloat16)
        product = jnp.dot(quintic, polynomial, preferred_element_type=jnp.float32)
        polynomial = (coeff_linear * polynomial.astype(jnp.float32) + product).astype(jnp.bfloat16)
    return polynomial

def final_update(polynomial, matrix, squared_norm):
    applied = jnp.dot(polynomial, matrix, preferred_element_type=jnp.float32)
    return (applied * (jnp.sqrt(jnp.float32(MODEL_D)) / jnp.sqrt(squared_norm + epsilon))).astype(jnp.bfloat16)

def reference(mom_values, mom_scale, gradients):
    summed = jnp.sum(jnp.square(gradients.astype(jnp.float32)))
    entries = MATS * EXPERT_FF * MODEL_D
    clip_factor = clip_level / jnp.sqrt(summed / entries + epsilon)

    def per_matrix(items):
        values, row_scale, gradient = items
        momentum = values.astype(jnp.float32) * row_scale[:, None]
        new_mom = (decay_rate * momentum + clip_factor * gradient.astype(jnp.float32)).astype(jnp.bfloat16)
        gram_matrix = jnp.dot(new_mom, new_mom.T, preferred_element_type=jnp.float32)
        squared_norm = jnp.trace(gram_matrix)
        polynomial = newton_chain(gram_matrix, squared_norm)
        return final_update(polynomial, new_mom, squared_norm)
    return lax.map(per_matrix, (mom_values, mom_scale, gradients))
```

```python
import jax
import jax.numpy as jnp
from jax import lax
from jax.experimental import pallas as pl
from jax.experimental.pallas import tpu as pltpu
from jax.sharding import Mesh
from jax.sharding import PartitionSpec as P

AXES = ("x", "core", "y", "z")
ZERO = ("x", "core")
EXPERT = ("y", "z")

coeff_linear = 3.4445
coeff_cubic = -4.775
coeff_quintic = 2.0315
decay_rate = 0.95
epsilon = 1e-06

WIDTH = 256
RAW = 1
REACH = 4

F32, BF16 = jnp.float32, jnp.bfloat16


def remote(src, dst, send_sem, recv_sem, **where):
    return pltpu.make_async_remote_copy(
        src_ref=src,
        dst_ref=dst,
        send_sem=send_sem,
        recv_sem=recv_sem,
        device_id=where,
        device_id_type=pl.DeviceIdType.MESH,
    )


def arrived(dst, recv_sem, send_sem, **where):
    remote(dst, dst, send_sem, recv_sem, **where).wait_recv()


def dot(a, b):
    return jnp.dot(a, b, preferred_element_type=F32)


def dot_t(a, b):
    return lax.dot_general(a, b, (((1,), (1,)), ((), ())), preferred_element_type=F32)


def near_offsets(n):
    if n <= 2 * REACH:
        return list(range(1, n))
    assert n == 4 * REACH
    return [o * s for o in range(REACH, 0, -1) for s in (1, -1)]


def kernel(
    entries, sizes,
    mv, ms, gr, out,
    gbuf, mbuf, xs_out, xs_in, ys_out, ys_in, zs_out, zs_in, far_out, far_in,
    ms_in, own_sc, src_sc, hop, d2, d1, xc, fresh, fresh_p, gram, g_out, g_in,
    n_ref, p_ref, c_ref, ubuf, uhop,
    loc_s, xs_s, ys_s, zs_s, far_s, ms_s, hop_s, d2_s, d1_s, f_s, fp_s, g_s, o_hop, o_d2, o_d1, o_p, o_own,
):
    ny, nz = sizes
    rows, half = gbuf.shape[2], gbuf.shape[3]
    chunks = half // WIDTH
    ff = 8 * rows
    x, c, y, z = (lax.axis_index(a) for a in AXES)
    xp, xm, x2 = lax.rem(x + 1, 4), lax.rem(x + 3, 4), lax.rem(x + 2, 4)
    other = 1 - c
    sides = (xp, xm)
    y_near, z_near = near_offsets(ny), near_offsets(nz)
    at_y = [lax.rem(y + (o + ny), ny) for o in y_near]
    at_z = [lax.rem(z + (o + nz), nz) for o in z_near]
    group = [(dx, dc) for dx in (2, 1, 3, 0) for dc in (0, 1) if dx or dc]

    def member(dx, dc):
        return {"x": lax.rem(x + dx, 4), "core": other if dc else c}

    barrier = pltpu.get_barrier_semaphore()
    for t in at_z:
        pl.semaphore_signal(barrier, inc=1, device_id={"z": t}, device_id_type=pl.DeviceIdType.MESH)
    for t in at_y:
        pl.semaphore_signal(barrier, inc=1, device_id={"y": t}, device_id_type=pl.DeviceIdType.MESH)
    for dx, dc in group:
        pl.semaphore_signal(barrier, inc=1, device_id=member(dx, dc), device_id_type=pl.DeviceIdType.MESH)

    local = [
        pltpu.make_async_copy(src.at[:, :, pl.ds(h * half, half)], dst.at[h], loc_s.at[t, h])
        for t, (src, dst) in enumerate(((gr, gbuf), (mv, mbuf)))
        for h in range(2)
    ]
    for copy in local:
        copy.start()

    acc = None
    for h in range(2):
        local[h].wait()
        for m in range(4):
            g = gbuf[h, m].astype(F32)
            part = jnp.sum((g * g).reshape(rows // 8, 8, half), axis=0)
            acc = part if acc is None else acc + part
    lanes = acc[:, :128]
    for i in range(1, half // 128):
        lanes = lanes + acc[:, i * 128 : (i + 1) * 128]
    xs_out[...] = jnp.sum(lanes, axis=0, keepdims=True)

    ii = lax.broadcasted_iota(jnp.int32, (rows, rows), 0)
    jj = lax.broadcasted_iota(jnp.int32, (rows, rows), 1)
    mat = lax.broadcasted_iota(jnp.int32, (4, rows), 0)

    def column(values, m):
        row = jnp.sum(jnp.where(mat == m, values, 0.0), axis=0, keepdims=True)
        col = jnp.sum(jnp.where(ii == jj, row, 0.0), axis=1, keepdims=True)
        return jnp.broadcast_to(decay_rate * col, (rows, WIDTH))

    own = ms[...]
    for i, m in enumerate((xp, xm, x)):
        own_sc[i] = column(own, m)

    pl.semaphore_wait(barrier, len(at_y) + len(at_z) + len(group))
    sent = []

    def send(*args, **where):
        copy = remote(*args, **where)
        copy.start()
        sent.append(copy)

    for dx, dc in group:
        i = 2 * dx + dc
        send(xs_out, xs_in.at[i], xs_s.at[0, i], xs_s.at[1, i], **member(dx, dc))
    for s, to in enumerate((xp, xm, x2)):
        for k in range(2):
            send(ms, ms_in.at[s, c], ms_s.at[0, s, k], ms_s.at[1, s, c], x=to, core=k)
    for t, src in enumerate((gr, mv)):
        for d in range(2):
            send(
                src.at[x2, :, pl.ds(d * half, half)], hop.at[t, d],
                hop_s.at[0, t, d], hop_s.at[1, t, d], x=sides[d], core=c,
            )
    if RAW:
        for t, src in enumerate((gr, mv)):
            for d in range(2):
                for k in range(2):
                    send(
                        src.at[sides[d], :, pl.ds(k * half, RAW * WIDTH)], d1.at[t, d, c],
                        d1_s.at[0, t, d, k], d1_s.at[1, t, d, c], x=sides[d], core=k,
                    )

    def forward(t):
        for d in range(2):
            arrived(hop.at[t, d], hop_s.at[1, t, d], hop_s.at[0, t, d], x=sides[d], core=c)
            send(hop.at[t, d], d2.at[t, c], d2_s.at[0, t, d], d2_s.at[1, t, c], x=sides[d], core=d)

    total = xs_out[...]
    for dx, dc in group:
        i = 2 * dx + dc
        arrived(xs_in.at[i], xs_s.at[1, i], xs_s.at[0, i], **member(dx, dc))
        total = total + xs_in[i]
    if y_near:
        ys_out[...] = total
        for i, t in enumerate(at_y):
            send(ys_out, ys_in.at[i], ys_s.at[0, i], ys_s.at[1, i], y=t)
    for s, to in enumerate((xp, xm, x2)):
        for k in range(2):
            arrived(ms_in.at[s, k], ms_s.at[1, s, k], ms_s.at[0, s, k], x=to, core=k)
            src_sc[s, k] = column(ms_in[s, k], x)
    forward(0)
    for i, t in enumerate(at_y):
        arrived(ys_in.at[i], ys_s.at[1, i], ys_s.at[0, i], y=t)
        total = total + ys_in[i]
    if z_near:
        zs_out[...] = total
        for i, t in enumerate(at_z):
            send(zs_out, zs_in.at[i], zs_s.at[0, i], zs_s.at[1, i], z=t)
    forward(1)
    ahead = behind = None
    for i, (o, t) in enumerate(zip(z_near, at_z)):
        arrived(zs_in.at[i], zs_s.at[1, i], zs_s.at[0, i], z=t)
        total = total + zs_in[i]
        if o < 0:
            ahead = zs_in[i] if ahead is None else ahead + zs_in[i]
        elif o < REACH:
            behind = zs_in[i] if behind is None else behind + zs_in[i]
    if nz > 2 * REACH:
        far_out[0] = ahead
        far_out[1] = behind
        for i, t in ((0, lax.rem(z + nz - REACH, nz)), (1, lax.rem(z + REACH, nz))):
            send(far_out.at[i], far_in.at[i], far_s.at[0, i], far_s.at[1, i], z=t)
        for i, t in ((0, lax.rem(z + REACH, nz)), (1, lax.rem(z + nz - REACH, nz))):
            arrived(far_in.at[i], far_s.at[1, i], far_s.at[0, i], z=t)
            total = total + far_in[i]
    clip = lax.rsqrt(jnp.sum(total, axis=1, keepdims=True) / entries + epsilon)

    def momentum(values, scale, gradient):
        return (values.astype(F32) * scale + clip * gradient.astype(F32)).astype(BF16)

    def cols(k):
        return pl.ds(k * WIDTH, WIDTH)

    for copy in local[2:]:
        copy.wait()
    my_rows = pl.ds(pl.multiple_of((2 * x + c) * rows, rows), rows)
    for k in range(RAW, chunks):
        for d in range(2):
            for h in range(2):
                fresh[k - RAW, d, h] = momentum(
                    mbuf[h, sides[d], :, cols(k)], own_sc[d], gbuf[h, sides[d], :, cols(k)]
                )
                send(
                    fresh.at[k - RAW, d, h], xc.at[k, my_rows],
                    f_s.at[0, k, d, h], f_s.at[1, k, d, c], x=sides[d], core=h,
                )
    for k in range(chunks):
        fresh_p[k] = momentum(mbuf[other, x, :, cols(k)], own_sc[2], gbuf[other, x, :, cols(k)])
    send(fresh_p, xc.at[:, my_rows], fp_s.at[0], fp_s.at[1], x=x, core=other)
    for k in range(chunks):
        xc[k, my_rows] = momentum(mbuf[c, x, :, cols(k)], own_sc[2], gbuf[c, x, :, cols(k)])

    def rows_of(chip, core):
        return pl.ds(pl.multiple_of((2 * chip + core) * rows, rows), rows)

    came = (xm, xp)
    for d in range(2):
        for k in range(2):
            if RAW:
                for t in range(2):
                    arrived(d1.at[t, d, k], d1_s.at[1, t, d, k], d1_s.at[0, t, d, k], x=sides[d], core=k)
                for i in range(RAW):
                    xc[i, rows_of(came[d], k)] = momentum(
                        d1[1, d, k, :, cols(i)], src_sc[d, k], d1[0, d, k, :, cols(i)]
                    )
    for k in range(2):
        for t in range(2):
            arrived(d2.at[t, k], d2_s.at[1, t, k], d2_s.at[0, t, k], x=xp, core=k)
        for i in range(chunks):
            xc[i, rows_of(x2, k)] = momentum(d2[1, k, :, cols(i)], src_sc[2, k], d2[0, k, :, cols(i)])
    arrived(xc.at[:, rows_of(x, other)], fp_s.at[1], fp_s.at[0], x=x, core=other)

    tall = ff // 2
    for k in range(chunks):
        if k >= RAW:
            for d in range(2):
                for h in range(2):
                    arrived(
                        xc.at[k, rows_of(came[d], h)], f_s.at[1, k, d, h], f_s.at[0, k, d, h],
                        x=sides[d], core=h,
                    )
        for r in range(2):
            part = dot_t(xc[k, pl.ds(r * tall, tall)], xc[k])
            if k:
                part = gram[pl.ds(r * tall, tall)] + part
            gram[pl.ds(r * tall, tall)] = part
            if k == chunks - 1:
                g_out[r] = part.astype(BF16)
                send(g_out.at[r], g_in.at[r], g_s.at[0, r], g_s.at[1, r], x=x, core=other)
    norm = None
    diag = lax.broadcasted_iota(jnp.int32, (128, 128), 0) == lax.broadcasted_iota(jnp.int32, (128, 128), 1)
    for r in range(2):
        arrived(g_in.at[r], g_s.at[1, r], g_s.at[0, r], x=x, core=other)
        whole = gram[pl.ds(r * tall, tall)] + g_in[r].astype(F32)
        gram[pl.ds(r * tall, tall)] = whole
        for b in range(tall // 128):
            square = whole[b * 128 : (b + 1) * 128, r * tall + b * 128 : r * tall + (b + 1) * 128]
            masked = jnp.where(diag, square, 0.0)
            norm = masked if norm is None else norm + masked
    norm = jnp.sum(jnp.sum(norm, axis=0, keepdims=True), axis=1, keepdims=True) + epsilon
    inverse = 1.0 / norm
    scale = (2.0 * half) ** 0.5 * lax.rsqrt(norm)

    for r in range(2):
        at = pl.ds(r * tall, tall)
        n_ref[at] = (gram[at] * inverse).astype(BF16)
    for r in range(2):
        at = pl.ds(r * tall, tall)
        eye = lax.broadcasted_iota(jnp.int32, (tall, ff), 0) + r * tall == lax.broadcasted_iota(jnp.int32, (tall, ff), 1)
        square = dot(n_ref[at], n_ref[...])
        p_ref[at] = (
            jnp.where(eye, coeff_linear, 0.0) + coeff_cubic * n_ref[at].astype(F32) + coeff_quintic * square
        ).astype(BF16)
    for r in range(2):
        at = pl.ds(r * tall, tall)
        halfway = dot(p_ref[at], n_ref[...]).astype(BF16)
        c_ref[at] = dot_t(halfway, p_ref[...]).astype(BF16)

    pair = 2 * rows
    mine = pl.ds(pl.multiple_of(c * half, half), half)
    theirs = pl.ds(pl.multiple_of(other * half, half), half)
    for i, chip in enumerate((x2, xp, xm, x)):
        at = pl.ds(pl.multiple_of(chip * pair, pair), pair)
        conj = c_ref[at]
        square = dot(conj, c_ref[...])
        quintic = (coeff_cubic * conj.astype(F32) + coeff_quintic * square).astype(BF16)
        product = dot(quintic, p_ref[...])
        final = (coeff_linear * p_ref[at].astype(F32) + product).astype(BF16)
        for k in range(chunks):
            u = (dot(final, xc[k]) * scale).astype(BF16)
            ubuf[i, 0, :, cols(k)] = u[:rows]
            ubuf[i, 1, :, cols(k)] = u[rows:]
        if i == 0:
            for d in range(2):
                send(ubuf.at[0, d], uhop.at[d], o_hop.at[0, d], o_hop.at[1, d], x=sides[d], core=c)
        elif i < 3:
            d = i - 1
            for h in range(2):
                send(
                    ubuf.at[i, h], out.at[x, :, mine],
                    o_d1.at[0, d, h], o_d1.at[1, d, c], x=sides[d], core=h,
                )
        else:
            send(ubuf.at[3, other], out.at[x, :, mine], o_p.at[0], o_p.at[1], x=x, core=other)
            stay = pltpu.make_async_copy(ubuf.at[3, c], out.at[x, :, mine], o_own)
            stay.start()
    for d in range(2):
        arrived(uhop.at[d], o_hop.at[1, d], o_hop.at[0, d], x=sides[d], core=c)
        send(uhop.at[d], out.at[came[d], :, mine], o_d2.at[0, d], o_d2.at[1, c], x=sides[d], core=d)
    stay.wait()
    arrived(out.at[x, :, theirs], o_p.at[1], o_p.at[0], x=x, core=other)
    for d in range(2):
        for h in range(2):
            arrived(
                out.at[came[d], :, pl.ds(h * half, half)], o_d1.at[1, d, h], o_d1.at[0, d, h],
                x=sides[d], core=h,
            )
    for h in range(2):
        arrived(out.at[x2, :, pl.ds(h * half, half)], o_d2.at[1, h], o_d2.at[0, h], x=xp, core=h)
    for copy in sent:
        copy.wait_send()


def per_device(mom_values, mom_scale, gradients):
    slots, rows, width = gradients.shape
    half, ff = width // 2, 8 * rows
    chunks = half // WIDTH
    sizes = (lax.axis_size("y"), lax.axis_size("z"))
    entries = float(gradients.size * 8 * sizes[0] * sizes[1])
    near = [max(len(near_offsets(n)), 1) for n in sizes]
    dma = pltpu.SemaphoreType.DMA

    def body(*refs):
        kernel(entries, sizes, *refs)

    return pl.pallas_call(
        body,
        out_shape=jax.ShapeDtypeStruct(mom_values.shape, BF16),
        in_specs=[
            pl.BlockSpec(memory_space=pl.ANY),
            pl.BlockSpec(memory_space=pltpu.VMEM),
            pl.BlockSpec(memory_space=pl.ANY),
        ],
        out_specs=pl.BlockSpec(memory_space=pltpu.VMEM),
        scratch_shapes=[
            pltpu.VMEM((2, slots, rows, half), BF16),
            pltpu.VMEM((2, slots, rows, half), BF16),
            pltpu.VMEM((1, 128), F32),
            pltpu.VMEM((8, 1, 128), F32),
            pltpu.VMEM((1, 128), F32),
            pltpu.VMEM((near[0], 1, 128), F32),
            pltpu.VMEM((1, 128), F32),
            pltpu.VMEM((near[1], 1, 128), F32),
            pltpu.VMEM((2, 1, 128), F32),
            pltpu.VMEM((2, 1, 128), F32),
            pltpu.VMEM((3, 2, slots, rows), F32),
            pltpu.VMEM((3, rows, WIDTH), F32),
            pltpu.VMEM((3, 2, rows, WIDTH), F32),
            pltpu.VMEM((2, 2, rows, half), BF16),
            pltpu.VMEM((2, 2, rows, half), BF16),
            pltpu.VMEM((2, 2, 2, rows, max(RAW, 1) * WIDTH), BF16),
            pltpu.VMEM((chunks, ff, WIDTH), BF16),
            pltpu.VMEM((chunks - RAW, 2, 2, rows, WIDTH), BF16),
            pltpu.VMEM((chunks, rows, WIDTH), BF16),
            pltpu.VMEM((ff, ff), F32),
            pltpu.VMEM((2, ff // 2, ff), BF16),
            pltpu.VMEM((2, ff // 2, ff), BF16),
            pltpu.VMEM((ff, ff), BF16),
            pltpu.VMEM((ff, ff), BF16),
            pltpu.VMEM((ff, ff), BF16),
            pltpu.VMEM((4, 2, rows, half), BF16),
            pltpu.VMEM((2, rows, half), BF16),
            dma((2, 2)),
            dma((2, 8)),
            dma((2, near[0])),
            dma((2, near[1])),
            dma((2, 2)),
            dma((2, 3, 2)),
            dma((2, 2, 2)),
            dma((2, 2, 2)),
            dma((2, 2, 2, 2)),
            dma((2, chunks, 2, 2)),
            dma((2,)),
            dma((2, 2)),
            dma((2, 2)),
            dma((2, 2)),
            dma((2, 2, 2)),
            dma((2,)),
            dma,
        ],
        compiler_params=pltpu.CompilerParams(
            collective_id=0, has_side_effects=True, vmem_limit_bytes=66_000_000
        ),
        name="muon",
    )(mom_values, mom_scale, gradients)


def solution(mesh):
    finer = Mesh(mesh.devices.reshape(4, 2, 8, 16), AXES)
    return jax.shard_map(
        per_device,
        mesh=finer,
        in_specs=(P(EXPERT, ZERO, None), P(EXPERT, ZERO), P(EXPERT, ZERO, None)),
        out_specs=P(EXPERT, ZERO, None),
        check_vma=False,
    )
```

```python
import jax
import jax.numpy as jnp
from jax import lax
from jax.experimental import pallas as pl
from jax.experimental.pallas import tpu as pltpu
from jax.sharding import Mesh
from jax.sharding import PartitionSpec as P

AXES = ("x", "core", "y", "z")
ZERO = ("x", "core")
EXPERT = ("y", "z")

coeff_linear = 3.4445
coeff_cubic = -4.775
coeff_quintic = 2.0315
decay_rate = 0.95
epsilon = 1e-06

WIDTH = 256
REACH = 4

STOP = 0
F32, BF16 = jnp.float32, jnp.bfloat16


def remote(src, dst, send_sem, recv_sem, **where):
    return pltpu.make_async_remote_copy(
        src_ref=src,
        dst_ref=dst,
        send_sem=send_sem,
        recv_sem=recv_sem,
        device_id=where,
        device_id_type=pl.DeviceIdType.MESH,
    )


def arrived(dst, recv_sem, send_sem, **where):
    remote(dst, dst, send_sem, recv_sem, **where).wait_recv()


def dot(a, b):
    return jnp.dot(a, b, preferred_element_type=F32)


def dot_t(a, b):
    return lax.dot_general(a, b, (((1,), (1,)), ((), ())), preferred_element_type=F32)


def near_offsets(n):
    if n <= 2 * REACH:
        return list(range(1, n))
    assert n == 4 * REACH
    return [o * s for o in range(REACH, 0, -1) for s in (1, -1)]


def kernel(
    entries, sizes,
    mv, ms, gr, out,
    gbuf, xs_out, xs_in, ys_out, ys_in, zs_out, zs_in, far_out, far_in, tot,
    ms_own, ms_in, sc, hop, raw, xc, gram, g_out, g_in, n_ref, p_ref, c_ref, ubuf, uhop,
    ready, loc_s, msl_s, xs_s, ys_s, zs_s, far_s, tot_s, ms_s, hop_s, fwd_s, d1_s, mate_s, raw_s, g_s,
    o_hop, o_d2, o_d1, o_p, o_own,
):
    ny, nz = sizes
    slots, rows = gbuf.shape[:2]
    half = raw.shape[3]
    chunks = half // WIDTH
    ff = 8 * rows
    x, c, y, z = (lax.axis_index(a) for a in AXES)
    xp, xm, x2 = lax.rem(x + 1, 4), lax.rem(x + 3, 4), lax.rem(x + 2, 4)
    other = 1 - c
    me = 2 * x + c
    sides = (xp, xm)
    came = (xm, xp)
    y_near, z_near = near_offsets(ny), near_offsets(nz)
    at_y = [lax.rem(y + (o + ny), ny) for o in y_near]
    at_z = [lax.rem(z + (o + nz), nz) for o in z_near]
    z_up, z_down = lax.rem(z + REACH, nz), lax.rem(z + nz - REACH % nz, nz)
    far = nz > 2 * REACH
    at_x = [lax.rem(x + dx, 4) for dx in range(4)]
    from_x = [lax.rem(x + 4 - dx, 4) for dx in range(4)]
    group = [(dx, dc) for dx in (2, 1, 3, 0) for dc in (0, 1) if dx or dc]
    mine = pl.ds(pl.multiple_of(c * half, half), half)
    theirs = pl.ds(pl.multiple_of(other * half, half), half)
    mesh_ids = pl.DeviceIdType.MESH

    def member(dx, dc):
        return {"x": at_x[dx], "core": other if dc else c}

    local = [pltpu.make_async_copy(gr.at[m], gbuf.at[m], loc_s.at[m]) for m in range(slots)]
    for copy in local:
        copy.start()
    barrier = pltpu.get_barrier_semaphore()
    for dx in (2, 1, 3, 0):

        @pl.when((c == 1) | (dx != 0))
        def _():
            pl.semaphore_signal(barrier, inc=1, device_id={"x": at_x[dx], "core": 0}, device_id_type=mesh_ids)

    @pl.when(c == 1)
    def _():
        for t in at_z:
            pl.semaphore_signal(barrier, inc=1, device_id={"z": t}, device_id_type=mesh_ids)
        for t in at_y:
            pl.semaphore_signal(barrier, inc=1, device_id={"y": t}, device_id_type=mesh_ids)

    scales = pltpu.make_async_copy(ms, ms_own, msl_s)
    scales.start()
    for t, src in enumerate((gr, mv)):
        pltpu.make_async_copy(src.at[x, :, mine], raw.at[t, me], raw_s.at[t, me]).start()

    @pl.when(c == 0)
    def _():
        pl.semaphore_wait(barrier, 7)
        pl.semaphore_signal(ready, inc=1, device_id={"core": 1}, device_id_type=mesh_ids)

    acc = None
    for m in range(slots):
        local[m].wait()
        for h in range(2):
            g = gbuf[m, :, h * half : (h + 1) * half].astype(F32)
            part = jnp.sum((g * g).reshape(rows // 8, 8, half), axis=0)
            acc = part if acc is None else acc + part
    lanes = acc[:, :128]
    for i in range(1, half // 128):
        lanes = lanes + acc[:, i * 128 : (i + 1) * 128]
    xs_out[...] = jnp.sum(lanes, axis=0, keepdims=True)

    @pl.when(c == 1)
    def _():
        pl.semaphore_wait(ready, 1)

    to_ones = [remote(xs_out, xs_in.at[2 * dx + c], xs_s.at[0, dx], xs_s.at[1, 2 * dx + c], x=at_x[dx], core=1) for dx in range(4)]
    to_scales = [
        remote(ms_own, ms_in.at[me], ms_s.at[0, 2 * dx + dc], ms_s.at[1, me], **member(dx, dc)) for dx, dc in group
    ]
    bulk = [
        remote(
            src.at[x2, :, pl.ds(d * half, half)], hop.at[t, d, c],
            hop_s.at[0, t, d, 0], hop_s.at[1, t, d, c], x=sides[d], core=0,
        )
        for t, src in enumerate((gr, mv))
        for d in range(2)
    ]
    for t, src in enumerate((gr, mv)):
        bulk.append(remote(src.at[x, :, theirs], raw.at[t, me], mate_s.at[t], raw_s.at[t, me], x=x, core=other))
        bulk.extend(
            remote(
                src.at[sides[d], :, pl.ds(k * half, half)], raw.at[t, me],
                d1_s.at[t, d, k], raw_s.at[t, me], x=sides[d], core=k,
            )
            for d in range(2)
            for k in range(2)
        )
    origin = [[2 * came[d] + k for k in range(2)] for d in range(2)]
    passed = [
        [
            remote(
                hop.at[t, d, k], raw.at[t, origin[d][k]],
                fwd_s.at[t, d, k], raw_s.at[t, origin[d][k]], x=sides[d], core=d,
            )
            for t in range(2)
            for d in range(2)
        ]
        for k in range(2)
    ]
    to_y = [remote(ys_out, ys_in.at[i], ys_s.at[0, i], ys_s.at[1, i], y=t) for i, t in enumerate(at_y)]
    to_z = [remote(zs_out, zs_in.at[i], zs_s.at[0, i], zs_s.at[1, i], z=t) for i, t in enumerate(at_z)]
    to_far = [
        remote(far_out.at[i], far_in.at[i], far_s.at[0, i], far_s.at[1, i], z=t) for i, t in ((0, z_down), (1, z_up))
    ]
    to_mate = remote(tot, tot, tot_s.at[0], tot_s.at[1], core=0)

    def start(copies):
        for copy in copies:
            copy.start()

    start(to_ones[1:])

    @pl.when(c == 0)
    def _():
        to_ones[0].start()

    scales.wait()
    start(to_scales)

    @pl.when((c == 0) | (2 * z < nz))
    def _():
        start(bulk)

    ii = lax.broadcasted_iota(jnp.int32, (rows, rows), 0)
    jj = lax.broadcasted_iota(jnp.int32, (rows, rows), 1)
    mat = lax.broadcasted_iota(jnp.int32, (slots, rows), 0)

    def column(values):
        row = jnp.sum(jnp.where(mat == x, values, 0.0), axis=0, keepdims=True)
        col = jnp.sum(jnp.where(ii == jj, row, 0.0), axis=1, keepdims=True)
        return jnp.broadcast_to(decay_rate * col, (rows, WIDTH))

    def columns():
        for dx, dc in group:
            i, at = 2 * dx + dc, member(dx, dc)
            who = 2 * at["x"] + at["core"]
            arrived(ms_in.at[who], ms_s.at[1, who], ms_s.at[0, i], **at)
            sc[who] = column(ms_in[who])
        sc[me] = column(ms_own[...])

    @pl.when(c == 1)
    def _():
        total = xs_out[...]
        for dx in range(4):
            for k in range(2):
                if dx or not k:
                    i = 2 * dx + k
                    arrived(xs_in.at[i], xs_s.at[1, i], xs_s.at[0, dx], x=from_x[dx], core=k)
                    total = total + xs_in[i]
        pl.semaphore_wait(barrier, len(at_y) + len(at_z))
        if y_near:
            ys_out[...] = total
            start(to_y)
            for i, t in enumerate(at_y):
                arrived(ys_in.at[i], ys_s.at[1, i], ys_s.at[0, i], y=t)
                total = total + ys_in[i]
        if z_near:
            zs_out[...] = total
            start(to_z)

        @pl.when(2 * z >= nz)
        def _():
            start(bulk)

        ahead = behind = None
        for i, (o, t) in enumerate(zip(z_near, at_z)):
            arrived(zs_in.at[i], zs_s.at[1, i], zs_s.at[0, i], z=t)
            total = total + zs_in[i]
            if o < 0:
                ahead = zs_in[i] if ahead is None else ahead + zs_in[i]
            elif o < REACH:
                behind = zs_in[i] if behind is None else behind + zs_in[i]
        if far:
            far_out[0] = ahead
            far_out[1] = behind
            start(to_far)
        columns()
        if far:
            for i, t in ((0, z_up), (1, z_down)):
                arrived(far_in.at[i], far_s.at[1, i], far_s.at[0, i], z=t)
                total = total + far_in[i]
        tot[...] = total
        to_mate.start()

    @pl.when(c == 0)
    def _():
        columns()
        for k in range(2):
            for i, copy in enumerate(passed[k]):
                t, d = i // 2, i % 2
                arrived(hop.at[t, d, k], hop_s.at[1, t, d, k], hop_s.at[0, t, d, 0], x=sides[d], core=0)
                copy.start()
        arrived(tot, tot_s.at[1], tot_s.at[0], core=1)

    clip = lax.rsqrt(jnp.sum(tot[...], axis=1, keepdims=True) / entries + epsilon)
    sent = to_ones[1:] + to_scales + bulk

    def send(*args, **where):
        copy = remote(*args, **where)
        copy.start()
        sent.append(copy)

    def finish():
        for copy in sent:
            copy.wait_send()

        @pl.when(c == 0)
        def _():
            for copy in to_ones[:1] + passed[0] + passed[1]:
                copy.wait_send()

        @pl.when(c == 1)
        def _():
            for copy in to_y + to_z + (to_far if far else []) + [to_mate]:
                copy.wait_send()

    if STOP == 4:
        for t in range(2):
            pltpu.make_async_copy(raw.at[t, me], raw.at[t, me], raw_s.at[t, me]).wait()
        out[0, :8, :128] = jnp.broadcast_to(clip, (8, 128)).astype(BF16)
        for i in range(8):
            for t in range(2):
                @pl.when(me != i)
                def _():
                    arrived(raw.at[t, i], raw_s.at[t, i], mate_s.at[t], x=xp, core=c)
        finish()
        return
    for i in range(8):
        for t in range(2):
            arrived(raw.at[t, i], raw_s.at[t, i], mate_s.at[t], x=xp, core=c)
    if STOP == 1:
        out[0, :8, :128] = jnp.broadcast_to(clip, (8, 128)).astype(BF16)
        finish()
        return

    tall = ff // 2
    for k in range(chunks):
        at = pl.ds(k * WIDTH, WIDTH)
        for i in range(8):
            xc[k, pl.ds(i * rows, rows)] = (
                raw[1, i, :, at].astype(F32) * sc[i] + clip * raw[0, i, :, at].astype(F32)
            ).astype(BF16)
        for r in range(2):
            part = dot_t(xc[k, pl.ds(r * tall, tall)], xc[k])
            if k:
                part = gram[pl.ds(r * tall, tall)] + part
            gram[pl.ds(r * tall, tall)] = part
            if k == chunks - 1:
                g_out[r] = part.astype(BF16)
                send(g_out.at[r], g_in.at[r], g_s.at[0, r], g_s.at[1, r], x=x, core=other)
    norm = None
    diag = lax.broadcasted_iota(jnp.int32, (128, 128), 0) == lax.broadcasted_iota(jnp.int32, (128, 128), 1)
    for r in range(2):
        arrived(g_in.at[r], g_s.at[1, r], g_s.at[0, r], x=x, core=other)
        whole = gram[pl.ds(r * tall, tall)] + g_in[r].astype(F32)
        gram[pl.ds(r * tall, tall)] = whole
        for b in range(tall // 128):
            square = whole[b * 128 : (b + 1) * 128, r * tall + b * 128 : r * tall + (b + 1) * 128]
            masked = jnp.where(diag, square, 0.0)
            norm = masked if norm is None else norm + masked
    norm = jnp.sum(jnp.sum(norm, axis=0, keepdims=True), axis=1, keepdims=True) + epsilon
    inverse = 1.0 / norm
    scale = (2.0 * half) ** 0.5 * lax.rsqrt(norm)

    if STOP == 2:
        out[0, :8, :128] = jnp.broadcast_to(inverse, (8, 128)).astype(BF16)
        finish()
        return
    for r in range(2):
        at = pl.ds(r * tall, tall)
        n_ref[at] = (gram[at] * inverse).astype(BF16)
    for r in range(2):
        at = pl.ds(r * tall, tall)
        eye = lax.broadcasted_iota(jnp.int32, (tall, ff), 0) + r * tall == lax.broadcasted_iota(jnp.int32, (tall, ff), 1)
        square = dot(n_ref[at], n_ref[...])
        p_ref[at] = (
            jnp.where(eye, coeff_linear, 0.0) + coeff_cubic * n_ref[at].astype(F32) + coeff_quintic * square
        ).astype(BF16)
    for r in range(2):
        at = pl.ds(r * tall, tall)
        halfway = dot(p_ref[at], n_ref[...]).astype(BF16)
        c_ref[at] = dot_t(halfway, p_ref[...]).astype(BF16)

    if STOP == 3:
        out[0, :8, :128] = (c_ref[:8, :128].astype(F32) * scale).astype(BF16)
        finish()
        return
    pair = 2 * rows

    def cols(k):
        return pl.ds(k * WIDTH, WIDTH)

    for i, chip in enumerate((x2, xp, xm, x)):
        at = pl.ds(pl.multiple_of(chip * pair, pair), pair)
        conj = c_ref[at]
        square = dot(conj, c_ref[...])
        quintic = (coeff_cubic * conj.astype(F32) + coeff_quintic * square).astype(BF16)
        product = dot(quintic, p_ref[...])
        final = (coeff_linear * p_ref[at].astype(F32) + product).astype(BF16)
        for k in range(chunks):
            u = (dot(final, xc[k]) * scale).astype(BF16)
            ubuf[i, 0, :, cols(k)] = u[:rows]
            ubuf[i, 1, :, cols(k)] = u[rows:]
        if i == 0:
            for d in range(2):
                send(ubuf.at[0, d], uhop.at[d], o_hop.at[0, d], o_hop.at[1, d], x=sides[d], core=c)
        elif i < 3:
            d = i - 1
            for h in range(2):
                send(
                    ubuf.at[i, h], out.at[x, :, mine],
                    o_d1.at[0, d, h], o_d1.at[1, d, c], x=sides[d], core=h,
                )
        else:
            send(ubuf.at[3, other], out.at[x, :, mine], o_p.at[0], o_p.at[1], x=x, core=other)
            stay = pltpu.make_async_copy(ubuf.at[3, c], out.at[x, :, mine], o_own)
            stay.start()
    for d in range(2):
        arrived(uhop.at[d], o_hop.at[1, d], o_hop.at[0, d], x=sides[d], core=c)
        send(uhop.at[d], out.at[came[d], :, mine], o_d2.at[0, d], o_d2.at[1, c], x=sides[d], core=d)
    stay.wait()
    arrived(out.at[x, :, theirs], o_p.at[1], o_p.at[0], x=x, core=other)
    for d in range(2):
        for h in range(2):
            arrived(
                out.at[came[d], :, pl.ds(h * half, half)], o_d1.at[1, d, h], o_d1.at[0, d, h],
                x=sides[d], core=h,
            )
    for h in range(2):
        arrived(out.at[x2, :, pl.ds(h * half, half)], o_d2.at[1, h], o_d2.at[0, h], x=xp, core=h)
    finish()


def per_device(mom_values, mom_scale, gradients):
    slots, rows, width = gradients.shape
    half, ff = width // 2, 8 * rows
    chunks = half // WIDTH
    sizes = (lax.axis_size("y"), lax.axis_size("z"))
    entries = float(gradients.size * 8 * sizes[0] * sizes[1])
    near = [max(len(near_offsets(n)), 1) for n in sizes]
    dma = pltpu.SemaphoreType.DMA

    def body(*refs):
        kernel(entries, sizes, *refs)

    return pl.pallas_call(
        body,
        out_shape=jax.ShapeDtypeStruct(mom_values.shape, BF16),
        in_specs=[pl.BlockSpec(memory_space=pltpu.HBM)] * 3,
        out_specs=pl.BlockSpec(memory_space=pltpu.VMEM),
        scratch_shapes=[
            pltpu.VMEM((slots, rows, width), BF16),
            pltpu.VMEM((1, 128), F32),
            pltpu.VMEM((8, 1, 128), F32),
            pltpu.VMEM((1, 128), F32),
            pltpu.VMEM((near[0], 1, 128), F32),
            pltpu.VMEM((1, 128), F32),
            pltpu.VMEM((near[1], 1, 128), F32),
            pltpu.VMEM((2, 1, 128), F32),
            pltpu.VMEM((2, 1, 128), F32),
            pltpu.VMEM((1, 128), F32),
            pltpu.VMEM((slots, rows), F32),
            pltpu.VMEM((8, slots, rows), F32),
            pltpu.VMEM((8, rows, WIDTH), F32),
            pltpu.VMEM((2, 2, 2, rows, half), BF16),
            pltpu.VMEM((2, 8, rows, half), BF16),
            pltpu.VMEM((chunks, ff, WIDTH), BF16),
            pltpu.VMEM((ff, ff), F32),
            pltpu.VMEM((2, ff // 2, ff), BF16),
            pltpu.VMEM((2, ff // 2, ff), BF16),
            pltpu.VMEM((ff, ff), BF16),
            pltpu.VMEM((ff, ff), BF16),
            pltpu.VMEM((ff, ff), BF16),
            pltpu.VMEM((4, 2, rows, half), BF16),
            pltpu.VMEM((2, rows, half), BF16),
            pltpu.SemaphoreType.REGULAR,
            dma((slots,)),
            dma,
            dma((2, 8)),
            dma((2, near[0])),
            dma((2, near[1])),
            dma((2, 2)),
            dma((2,)),
            dma((2, 8)),
            dma((2, 2, 2, 2)),
            dma((2, 2, 2)),
            dma((2, 2, 2)),
            dma((2,)),
            dma((2, 8)),
            dma((2, 2)),
            dma((2, 2)),
            dma((2, 2)),
            dma((2, 2, 2)),
            dma((2,)),
            dma,
        ],
        compiler_params=pltpu.CompilerParams(
            collective_id=0, has_side_effects=True, vmem_limit_bytes=66_000_000
        ),
        name="muon",
    )(mom_values, mom_scale, gradients)


def solution(mesh):
    finer = Mesh(mesh.devices.reshape(4, 2, 8, 16), AXES)
    return jax.shard_map(
        per_device,
        mesh=finer,
        in_specs=(P(EXPERT, ZERO, None), P(EXPERT, ZERO), P(EXPERT, ZERO, None)),
        out_specs=P(EXPERT, ZERO, None),
        check_vma=False,
    )
```

```python
import jax
import jax.numpy as jnp
from jax import lax
from jax.experimental import pallas as pl
from jax.experimental.pallas import tpu as pltpu
from jax.sharding import Mesh
from jax.sharding import PartitionSpec as P

AXES = ("x", "core", "y", "z")
ZERO = ("x", "core")
EXPERT = ("y", "z")

coeff_linear = 3.4445
coeff_cubic = -4.775
coeff_quintic = 2.0315
decay_rate = 0.95
epsilon = 1e-06

WIDTH = 256
STOP = 0
REACH = 4
F32, BF16 = jnp.float32, jnp.bfloat16


def remote(src, dst, send_sem, recv_sem, **where):
    return pltpu.make_async_remote_copy(
        src_ref=src,
        dst_ref=dst,
        send_sem=send_sem,
        recv_sem=recv_sem,
        device_id=where,
        device_id_type=pl.DeviceIdType.MESH,
    )


def arrived(dst, recv_sem, send_sem, **where):
    remote(dst, dst, send_sem, recv_sem, **where).wait_recv()


def dot(a, b):
    return jnp.dot(a, b, preferred_element_type=F32)


def dot_t(a, b):
    return lax.dot_general(a, b, (((1,), (1,)), ((), ())), preferred_element_type=F32)


def far_first(n):
    if n > 2 * REACH:
        assert n == 4 * REACH
        return [o * s for o in range(REACH, 0, -1) for s in (1, -1)]
    return sorted(range(1, n), key=lambda o: -min(o, n - o))


def kernel(
    entries, sizes,
    mv, ms, gr, out,
    gbuf, xs_out, xs_in, ys_out, ys_in, zs_out, zs_in, far_out, far_in, tot,
    ms_own, ms_in, sc, hop, raw, xc, gram, g_out, g_in, n_ref, p_ref, c_ref, ubuf, uhop,
    ready, late, loc_s, msl_s, xs_s, ys_s, zs_s, far_s, tot_s, ms_s, hop_s, fwd_s, d1_s, mate_s, raw_s, g_s,
    o_hop, o_d2, o_d1, o_p, o_own,
):
    ny, nz = sizes
    slots, rows = gbuf.shape[:2]
    half = raw.shape[3]
    chunks = half // WIDTH
    ff = 8 * rows
    x, c, y, z = (lax.axis_index(a) for a in AXES)
    xp, xm, x2 = lax.rem(x + 1, 4), lax.rem(x + 3, 4), lax.rem(x + 2, 4)
    other = 1 - c
    me = 2 * x + c
    sides = (xp, xm)
    came = (xm, xp)
    y_near, z_near = far_first(ny), far_first(nz)
    at_y = [lax.rem(y + (o + ny), ny) for o in y_near]
    at_z = [lax.rem(z + (o + nz), nz) for o in z_near]
    z_up, z_down = lax.rem(z + REACH, nz), lax.rem(z + nz - REACH % nz, nz)
    far = nz > 2 * REACH
    at_x = [lax.rem(x + dx, 4) for dx in range(4)]
    from_x = [lax.rem(x + 4 - dx, 4) for dx in range(4)]
    group = [(dx, dc) for dx in (2, 1, 3, 0) for dc in (0, 1) if dx or dc]
    mine = pl.ds(pl.multiple_of(c * half, half), half)
    theirs = pl.ds(pl.multiple_of(other * half, half), half)
    mesh_ids = pl.DeviceIdType.MESH

    def member(dx, dc):
        return {"x": at_x[dx], "core": other if dc else c}

    barrier = pltpu.get_barrier_semaphore()
    for dx in (2, 1, 3, 0):

        @pl.when(((c == 1) | (dx != 0)) & (me != 0))
        def _():
            pl.semaphore_signal(barrier, inc=1, device_id={"x": at_x[dx], "core": 0}, device_id_type=mesh_ids)

    local = [pltpu.make_async_copy(gr.at[m], gbuf.at[m], loc_s.at[m]) for m in range(slots)]
    for copy in local:
        copy.start()
    @pl.when(c == 1)
    def _():
        for t in at_z:
            pl.semaphore_signal(barrier, inc=1, device_id={"z": t}, device_id_type=mesh_ids)
        for t in at_y:
            pl.semaphore_signal(barrier, inc=1, device_id={"y": t}, device_id_type=mesh_ids)

    scales = pltpu.make_async_copy(ms, ms_own, msl_s)
    scales.start()
    for t, src in enumerate((gr, mv)):
        pltpu.make_async_copy(src.at[x, :, mine], raw.at[t, me], raw_s.at[t, me]).start()

    @pl.when(c == 0)
    def _():
        pl.semaphore_wait(barrier, jnp.where(x == 0, 7, 6))

        @pl.when(x == 0)
        def _():
            for dx, dc in group:
                pl.semaphore_signal(late, inc=1, device_id=member(dx, dc), device_id_type=mesh_ids)

        @pl.when(x != 0)
        def _():
            pl.semaphore_signal(ready, inc=1, device_id={"core": 1}, device_id_type=mesh_ids)

        @pl.when(x == 1)
        def _():
            pl.semaphore_signal(ready, inc=1, device_id={"x": xm, "core": 1}, device_id_type=mesh_ids)

    acc = None
    for m in range(slots):
        local[m].wait()
        for h in range(2):
            g = gbuf[m, :, h * half : (h + 1) * half].astype(F32)
            part = jnp.sum((g * g).reshape(rows // 8, 8, half), axis=0)
            acc = part if acc is None else acc + part
    lanes = acc[:, :128]
    for i in range(1, half // 128):
        lanes = lanes + acc[:, i * 128 : (i + 1) * 128]
    xs_out[...] = jnp.sum(lanes, axis=0, keepdims=True)

    @pl.when(c == 1)
    def _():
        pl.semaphore_wait(ready, 1)

    to_ones = [remote(xs_out, xs_in.at[2 * dx + c], xs_s.at[0, dx], xs_s.at[1, 2 * dx + c], x=at_x[dx], core=1) for dx in range(4)]
    to_scales = [
        (
            remote(ms_own, ms_in.at[me], ms_s.at[0, 2 * dx + dc], ms_s.at[1, me], **member(dx, dc)),
            (at_x[dx] == 0) & ((c == 1) if dc else (c == 0)),
        )
        for dx, dc in group
    ]
    bulk = [
        (
            remote(
                src.at[x2, :, pl.ds(d * half, half)], hop.at[t, d, c],
                hop_s.at[0, t, d, 0], hop_s.at[1, t, d, c], x=sides[d], core=0,
            ),
            sides[d] == 0,
        )
        for t, src in enumerate((gr, mv))
        for d in range(2)
    ]
    for t, src in enumerate((gr, mv)):
        mate = remote(src.at[x, :, theirs], raw.at[t, me], mate_s.at[t], raw_s.at[t, me], x=x, core=other)
        bulk.append((mate, me == 1))
        for d in range(2):
            for k in range(2):
                copy = remote(
                    src.at[sides[d], :, pl.ds(k * half, half)], raw.at[t, me],
                    d1_s.at[t, d, k], raw_s.at[t, me], x=sides[d], core=k,
                )
                bulk.append((copy, sides[d] == 0 if k == 0 else None))
    origin = [[2 * came[d] + k for k in range(2)] for d in range(2)]
    passed = [
        [
            remote(
                hop.at[t, d, k], raw.at[t, origin[d][k]],
                fwd_s.at[t, d, k], raw_s.at[t, origin[d][k]], x=sides[d], core=d,
            )
            for t in range(2)
            for d in range(2)
        ]
        for k in range(2)
    ]
    to_y = [remote(ys_out, ys_in.at[i], ys_s.at[0, i], ys_s.at[1, i], y=t) for i, t in enumerate(at_y)]
    to_z = [remote(zs_out, zs_in.at[i], zs_s.at[0, i], zs_s.at[1, i], z=t) for i, t in enumerate(at_z)]
    to_far = [
        remote(far_out.at[i], far_in.at[i], far_s.at[0, i], far_s.at[1, i], z=t) for i, t in ((0, z_down), (1, z_up))
    ]
    to_mate = remote(tot, tot, tot_s.at[0], tot_s.at[1], core=0)

    def start(copies):
        for copy in copies:
            copy.start()

    def start_known(copies):
        for copy, to_late in copies:
            if to_late is None:
                copy.start()
            else:
                pl.when(jnp.logical_not(to_late))(copy.start)

    def start_late(copies):
        for copy, to_late in copies:
            if to_late is not None:
                pl.when(to_late)(copy.start)

    def wait_late():
        @pl.when(me != 0)
        def _():
            pl.semaphore_wait(late, 1)

    start(to_ones[1:])

    @pl.when(c == 0)
    def _():
        to_ones[0].start()

    scales.wait()
    start_known(to_scales)

    @pl.when((c == 0) | (2 * z < nz))
    def _():
        start_known(bulk)

    ii = lax.broadcasted_iota(jnp.int32, (rows, rows), 0)
    jj = lax.broadcasted_iota(jnp.int32, (rows, rows), 1)
    mat = lax.broadcasted_iota(jnp.int32, (slots, rows), 0)

    def column(values):
        row = jnp.sum(jnp.where(mat == x, values, 0.0), axis=0, keepdims=True)
        col = jnp.sum(jnp.where(ii == jj, row, 0.0), axis=1, keepdims=True)
        return jnp.broadcast_to(decay_rate * col, (rows, WIDTH))

    def columns():
        for dx, dc in group:
            i, at = 2 * dx + dc, member(dx, dc)
            who = 2 * at["x"] + at["core"]
            arrived(ms_in.at[who], ms_s.at[1, who], ms_s.at[0, i], **at)
            sc[who] = column(ms_in[who])
        sc[me] = column(ms_own[...])

    @pl.when(c == 1)
    def _():
        total = xs_out[...]
        for dx in range(4):
            for k in range(2):
                if dx or not k:
                    i = 2 * dx + k
                    arrived(xs_in.at[i], xs_s.at[1, i], xs_s.at[0, dx], x=from_x[dx], core=k)
                    total = total + xs_in[i]
        pl.semaphore_wait(barrier, len(at_y) + len(at_z))
        if y_near:
            ys_out[...] = total
            start(to_y)
            for i, t in enumerate(at_y):
                arrived(ys_in.at[i], ys_s.at[1, i], ys_s.at[0, i], y=t)
                total = total + ys_in[i]
        zs_out[...] = total
        start(to_z)

        wait_late()
        start_late(to_scales)

        @pl.when(2 * z < nz)
        def _():
            start_late(bulk)

        @pl.when(2 * z >= nz)
        def _():
            start([copy for copy, _ in bulk])

        ahead = behind = None
        for i, (o, t) in enumerate(zip(z_near, at_z)):
            arrived(zs_in.at[i], zs_s.at[1, i], zs_s.at[0, i], z=t)
            total = total + zs_in[i]
            if o < 0:
                ahead = zs_in[i] if ahead is None else ahead + zs_in[i]
            elif o < REACH:
                behind = zs_in[i] if behind is None else behind + zs_in[i]
        if far:
            far_out[0] = ahead
            far_out[1] = behind
            start(to_far)
        columns()
        if far:
            for i, t in ((0, z_up), (1, z_down)):
                arrived(far_in.at[i], far_s.at[1, i], far_s.at[0, i], z=t)
                total = total + far_in[i]
        tot[...] = total
        to_mate.start()

    @pl.when(c == 0)
    def _():
        wait_late()
        start_late(to_scales + bulk)
        columns()
        for k in range(2):
            for i, copy in enumerate(passed[k]):
                t, d = i // 2, i % 2
                arrived(hop.at[t, d, k], hop_s.at[1, t, d, k], hop_s.at[0, t, d, 0], x=sides[d], core=0)
                copy.start()
        arrived(tot, tot_s.at[1], tot_s.at[0], core=1)

    clip = lax.rsqrt(jnp.sum(tot[...], axis=1, keepdims=True) / entries + epsilon)
    sent = to_ones[1:] + [copy for copy, _ in to_scales + bulk]

    def send(*args, **where):
        copy = remote(*args, **where)
        copy.start()
        sent.append(copy)

    def finish():
        for copy in sent:
            copy.wait_send()

        @pl.when(c == 0)
        def _():
            for copy in to_ones[:1] + passed[0] + passed[1]:
                copy.wait_send()

        @pl.when(c == 1)
        def _():
            for copy in to_y + to_z + (to_far if far else []) + [to_mate]:
                copy.wait_send()

    if STOP == 4:
        for t in range(2):
            pltpu.make_async_copy(raw.at[t, me], raw.at[t, me], raw_s.at[t, me]).wait()
        out[0, :8, :128] = jnp.broadcast_to(clip, (8, 128)).astype(BF16)
        for i in range(8):
            for t in range(2):
                @pl.when(me != i)
                def _():
                    arrived(raw.at[t, i], raw_s.at[t, i], mate_s.at[t], x=xp, core=c)
        finish()
        return
    for i in range(8):
        for t in range(2):
            arrived(raw.at[t, i], raw_s.at[t, i], mate_s.at[t], x=xp, core=c)
    if STOP == 1:
        out[0, :8, :128] = jnp.broadcast_to(clip, (8, 128)).astype(BF16)
        finish()
        return

    tall = ff // 2
    for k in range(chunks):
        at = pl.ds(k * WIDTH, WIDTH)
        for i in range(8):
            xc[k, pl.ds(i * rows, rows)] = (
                raw[1, i, :, at].astype(F32) * sc[i] + clip * raw[0, i, :, at].astype(F32)
            ).astype(BF16)
        for r in range(2):
            part = dot_t(xc[k, pl.ds(r * tall, tall)], xc[k])
            if k:
                part = gram[pl.ds(r * tall, tall)] + part
            gram[pl.ds(r * tall, tall)] = part
            if k == chunks - 1:
                g_out[r] = part.astype(BF16)
                send(g_out.at[r], g_in.at[r], g_s.at[0, r], g_s.at[1, r], x=x, core=other)
    norm = None
    diag = lax.broadcasted_iota(jnp.int32, (128, 128), 0) == lax.broadcasted_iota(jnp.int32, (128, 128), 1)
    for r in range(2):
        arrived(g_in.at[r], g_s.at[1, r], g_s.at[0, r], x=x, core=other)
        whole = gram[pl.ds(r * tall, tall)] + g_in[r].astype(F32)
        gram[pl.ds(r * tall, tall)] = whole
        for b in range(tall // 128):
            square = whole[b * 128 : (b + 1) * 128, r * tall + b * 128 : r * tall + (b + 1) * 128]
            masked = jnp.where(diag, square, 0.0)
            norm = masked if norm is None else norm + masked
    norm = jnp.sum(jnp.sum(norm, axis=0, keepdims=True), axis=1, keepdims=True) + epsilon
    inverse = 1.0 / norm
    scale = (2.0 * half) ** 0.5 * lax.rsqrt(norm)

    if STOP == 2:
        out[0, :8, :128] = jnp.broadcast_to(inverse, (8, 128)).astype(BF16)
        finish()
        return
    for r in range(2):
        at = pl.ds(r * tall, tall)
        n_ref[at] = (gram[at] * inverse).astype(BF16)
    for r in range(2):
        at = pl.ds(r * tall, tall)
        eye = lax.broadcasted_iota(jnp.int32, (tall, ff), 0) + r * tall == lax.broadcasted_iota(jnp.int32, (tall, ff), 1)
        square = dot(n_ref[at], n_ref[...])
        p_ref[at] = (
            jnp.where(eye, coeff_linear, 0.0) + coeff_cubic * n_ref[at].astype(F32) + coeff_quintic * square
        ).astype(BF16)
    for r in range(2):
        at = pl.ds(r * tall, tall)
        halfway = dot(p_ref[at], n_ref[...]).astype(BF16)
        c_ref[at] = dot_t(halfway, p_ref[...]).astype(BF16)

    if STOP == 3:
        out[0, :8, :128] = (c_ref[:8, :128].astype(F32) * scale).astype(BF16)
        finish()
        return
    pair = 2 * rows

    def cols(k):
        return pl.ds(k * WIDTH, WIDTH)

    for i, chip in enumerate((x2, xp, xm, x)):
        at = pl.ds(pl.multiple_of(chip * pair, pair), pair)
        conj = c_ref[at]
        square = dot(conj, c_ref[...])
        quintic = (coeff_cubic * conj.astype(F32) + coeff_quintic * square).astype(BF16)
        product = dot(quintic, p_ref[...])
        final = (coeff_linear * p_ref[at].astype(F32) + product).astype(BF16)
        for k in range(chunks):
            u = (dot(final, xc[k]) * scale).astype(BF16)
            ubuf[i, 0, :, cols(k)] = u[:rows]
            ubuf[i, 1, :, cols(k)] = u[rows:]
        if i == 0:
            for d in range(2):
                send(ubuf.at[0, d], uhop.at[d], o_hop.at[0, d], o_hop.at[1, d], x=sides[d], core=c)
        elif i < 3:
            d = i - 1
            for h in range(2):
                send(
                    ubuf.at[i, h], out.at[x, :, mine],
                    o_d1.at[0, d, h], o_d1.at[1, d, c], x=sides[d], core=h,
                )
        else:
            send(ubuf.at[3, other], out.at[x, :, mine], o_p.at[0], o_p.at[1], x=x, core=other)
            stay = pltpu.make_async_copy(ubuf.at[3, c], out.at[x, :, mine], o_own)
            stay.start()
    for d in range(2):
        arrived(uhop.at[d], o_hop.at[1, d], o_hop.at[0, d], x=sides[d], core=c)
        send(uhop.at[d], out.at[came[d], :, mine], o_d2.at[0, d], o_d2.at[1, c], x=sides[d], core=d)
    stay.wait()
    arrived(out.at[x, :, theirs], o_p.at[1], o_p.at[0], x=x, core=other)
    for d in range(2):
        for h in range(2):
            arrived(
                out.at[came[d], :, pl.ds(h * half, half)], o_d1.at[1, d, h], o_d1.at[0, d, h],
                x=sides[d], core=h,
            )
    for h in range(2):
        arrived(out.at[x2, :, pl.ds(h * half, half)], o_d2.at[1, h], o_d2.at[0, h], x=xp, core=h)
    finish()


def per_device(mom_values, mom_scale, gradients):
    slots, rows, width = gradients.shape
    half, ff = width // 2, 8 * rows
    chunks = half // WIDTH
    sizes = (lax.axis_size("y"), lax.axis_size("z"))
    entries = float(gradients.size * 8 * sizes[0] * sizes[1])
    near = [max(len(far_first(n)), 1) for n in sizes]
    dma = pltpu.SemaphoreType.DMA

    def body(*refs):
        kernel(entries, sizes, *refs)

    return pl.pallas_call(
        body,
        out_shape=jax.ShapeDtypeStruct(mom_values.shape, BF16),
        in_specs=[pl.BlockSpec(memory_space=pltpu.HBM)] * 3,
        out_specs=pl.BlockSpec(memory_space=pltpu.VMEM),
        scratch_shapes=[
            pltpu.VMEM((slots, rows, width), BF16),
            pltpu.VMEM((1, 128), F32),
            pltpu.VMEM((8, 1, 128), F32),
            pltpu.VMEM((1, 128), F32),
            pltpu.VMEM((near[0], 1, 128), F32),
            pltpu.VMEM((1, 128), F32),
            pltpu.VMEM((near[1], 1, 128), F32),
            pltpu.VMEM((2, 1, 128), F32),
            pltpu.VMEM((2, 1, 128), F32),
            pltpu.VMEM((1, 128), F32),
            pltpu.VMEM((slots, rows), F32),
            pltpu.VMEM((8, slots, rows), F32),
            pltpu.VMEM((8, rows, WIDTH), F32),
            pltpu.VMEM((2, 2, 2, rows, half), BF16),
            pltpu.VMEM((2, 8, rows, half), BF16),
            pltpu.VMEM((chunks, ff, WIDTH), BF16),
            pltpu.VMEM((ff, ff), F32),
            pltpu.VMEM((2, ff // 2, ff), BF16),
            pltpu.VMEM((2, ff // 2, ff), BF16),
            pltpu.VMEM((ff, ff), BF16),
            pltpu.VMEM((ff, ff), BF16),
            pltpu.VMEM((ff, ff), BF16),
            pltpu.VMEM((4, 2, rows, half), BF16),
            pltpu.VMEM((2, rows, half), BF16),
            pltpu.SemaphoreType.REGULAR,
            pltpu.SemaphoreType.REGULAR,
            dma((slots,)),
            dma,
            dma((2, 8)),
            dma((2, near[0])),
            dma((2, near[1])),
            dma((2, 2)),
            dma((2,)),
            dma((2, 8)),
            dma((2, 2, 2, 2)),
            dma((2, 2, 2)),
            dma((2, 2, 2)),
            dma((2,)),
            dma((2, 8)),
            dma((2, 2)),
            dma((2, 2)),
            dma((2, 2)),
            dma((2, 2, 2)),
            dma((2,)),
            dma,
        ],
        compiler_params=pltpu.CompilerParams(
            collective_id=0, has_side_effects=True, vmem_limit_bytes=55_200_000
        ),
        name="muon",
    )(mom_values, mom_scale, gradients)


def solution(mesh):
    finer = Mesh(mesh.devices.reshape(4, 2, 8, 16), AXES)
    return jax.shard_map(
        per_device,
        mesh=finer,
        in_specs=(P(EXPERT, ZERO, None), P(EXPERT, ZERO), P(EXPERT, ZERO, None)),
        out_specs=P(EXPERT, ZERO, None),
        check_vma=False,
    )
```

```python
import jax
import jax.numpy as jnp
from jax import lax
from jax.experimental import pallas as pl
from jax.experimental.pallas import tpu as pltpu
from jax.sharding import Mesh
from jax.sharding import PartitionSpec as P

AXES = ("x", "core", "y", "z")
ZERO = ("x", "core")
EXPERT = ("y", "z")

coeff_linear = 3.4445
coeff_cubic = -4.775
coeff_quintic = 2.0315
decay_rate = 0.95
epsilon = 1e-06

WIDTH = 256
REACH = 4
F32, BF16 = jnp.float32, jnp.bfloat16


def remote(src, dst, send_sem, recv_sem, **where):
    return pltpu.make_async_remote_copy(
        src_ref=src,
        dst_ref=dst,
        send_sem=send_sem,
        recv_sem=recv_sem,
        device_id=where,
        device_id_type=pl.DeviceIdType.MESH,
    )


def arrived(dst, recv_sem, send_sem, **where):
    remote(dst, dst, send_sem, recv_sem, **where).wait_recv()


def dot(a, b):
    return jnp.dot(a, b, preferred_element_type=F32)


def dot_t(a, b):
    return lax.dot_general(a, b, (((1,), (1,)), ((), ())), preferred_element_type=F32)


def far_first(n):
    if n > 2 * REACH:
        assert n == 4 * REACH
        return [o * s for o in range(REACH, 0, -1) for s in (1, -1)]
    return sorted(range(1, n), key=lambda o: -min(o, n - o))


def kernel(
    entries, sizes,
    mv, ms, gr, out,
    gbuf, xs_out, xs_in, ys_out, ys_in, zs_out, zs_in, far_out, far_in, tot,
    ms_own, ms_in, sc, hop, raw, xc, gram, g_out, g_in, n_ref, p_ref, c_ref, ubuf, uhop, counted,
    ready, late, loc_s, msl_s, sum_send, xs_s, ys_s, zs_s, far_s, tot_s, ms_send, ms_s, bulk_send, hop_s, fwd_send,
    raw_s, g_s, o_send, o_mate, o_hop, o_s,
):
    ny, nz = sizes
    slots, rows = gbuf.shape[:2]
    half = raw.shape[3]
    chunks = half // WIDTH
    ff = 8 * rows
    x, c, y, z = (lax.axis_index(a) for a in AXES)
    xp, xm, x2 = lax.rem(x + 1, 4), lax.rem(x + 3, 4), lax.rem(x + 2, 4)
    other = 1 - c
    me = 2 * x + c
    sides = (xp, xm)
    came = (xm, xp)
    y_near, z_near = far_first(ny), far_first(nz)
    at_y = [lax.rem(y + (o + ny), ny) for o in y_near]
    at_z = [lax.rem(z + (o + nz), nz) for o in z_near]
    z_up, z_down = lax.rem(z + REACH, nz), lax.rem(z + nz - REACH % nz, nz)
    far = nz > 2 * REACH
    at_x = [lax.rem(x + dx, 4) for dx in range(4)]
    from_x = [lax.rem(x + 4 - dx, 4) for dx in range(4)]
    group = [(dx, dc) for dx in (2, 1, 3, 0) for dc in (0, 1) if dx or dc]
    mine = pl.ds(pl.multiple_of(c * half, half), half)
    theirs = pl.ds(pl.multiple_of(other * half, half), half)
    mesh_ids = pl.DeviceIdType.MESH

    def member(dx, dc):
        return {"x": at_x[dx], "core": other if dc else c}

    barrier = pltpu.get_barrier_semaphore()
    for dx in (2, 1, 3, 0):

        @pl.when(((c == 1) | (dx != 0)) & (me != 0))
        def _():
            pl.semaphore_signal(barrier, inc=1, device_id={"x": at_x[dx], "core": 0}, device_id_type=mesh_ids)

    local = [pltpu.make_async_copy(gr.at[m], gbuf.at[m], loc_s.at[m]) for m in range(slots)]
    for copy in local:
        copy.start()
    if far:

        @pl.when(c == 0)
        def _():
            for t in (z_up, z_down):
                pl.semaphore_signal(barrier, inc=1, device_id={"z": t, "core": 1}, device_id_type=mesh_ids)

    @pl.when(c == 1)
    def _():
        for t in at_z:
            pl.semaphore_signal(barrier, inc=1, device_id={"z": t}, device_id_type=mesh_ids)
        for t in at_y:
            pl.semaphore_signal(barrier, inc=1, device_id={"y": t}, device_id_type=mesh_ids)

    scales = pltpu.make_async_copy(ms, ms_own, msl_s)
    scales.start()
    pltpu.make_async_copy(ms, ms_in.at[me], ms_s).start()
    for t, src in enumerate((gr, mv)):
        pltpu.make_async_copy(src.at[x, :, mine], raw.at[t, me], raw_s).start()

    @pl.when(c == 0)
    def _():
        pl.semaphore_wait(barrier, jnp.where(x == 0, 7, 6))

        @pl.when(x == 0)
        def _():
            for dx, dc in group:
                pl.semaphore_signal(late, inc=1, device_id=member(dx, dc), device_id_type=mesh_ids)

        @pl.when(x != 0)
        def _():
            pl.semaphore_signal(ready, inc=1, device_id={"core": 1}, device_id_type=mesh_ids)

        @pl.when(x == 1)
        def _():
            pl.semaphore_signal(ready, inc=1, device_id={"x": xm, "core": 1}, device_id_type=mesh_ids)

    acc = None
    for m in range(slots):
        local[m].wait()
        for h in range(2):
            g = gbuf[m, :, h * half : (h + 1) * half].astype(F32)
            part = jnp.sum((g * g).reshape(rows // 8, 8, half), axis=0)
            acc = part if acc is None else acc + part
    lanes = acc[:, :128]
    for i in range(1, half // 128):
        lanes = lanes + acc[:, i * 128 : (i + 1) * 128]
    xs_out[...] = jnp.sum(lanes, axis=0, keepdims=True)

    @pl.when(c == 1)
    def _():
        pl.semaphore_wait(ready, 1)

    to_ones = [remote(xs_out, xs_in.at[2 * ((dx + 3) % 4) + c], sum_send, xs_s, x=at_x[dx], core=1) for dx in range(4)]
    to_scales = [
        (
            remote(ms_own, ms_in.at[me], ms_send, ms_s, **member(dx, dc)),
            (at_x[dx] == 0) & ((c == 1) if dc else (c == 0)),
        )
        for dx, dc in group
    ]
    bulk = [
        (
            remote(
                src.at[x2, :, pl.ds(d * half, half)], hop.at[t, d, c],
                bulk_send, hop_s.at[c], x=sides[d], core=0,
            ),
            sides[d] == 0,
        )
        for t, src in enumerate((gr, mv))
        for d in range(2)
    ]
    for t, src in enumerate((gr, mv)):
        mate = remote(src.at[x, :, theirs], raw.at[t, me], bulk_send, raw_s, x=x, core=other)
        bulk.append((mate, me == 1))
        for d in range(2):
            for k in range(2):
                copy = remote(
                    src.at[sides[d], :, pl.ds(k * half, half)], raw.at[t, me],
                    bulk_send, raw_s, x=sides[d], core=k,
                )
                bulk.append((copy, sides[d] == 0 if k == 0 else None))
    origin = [[2 * came[d] + k for k in range(2)] for d in range(2)]
    passed = [
        [
            remote(
                hop.at[t, d, k], raw.at[t, origin[d][k]],
                fwd_send, raw_s, x=sides[d], core=d,
            )
            for t in range(2)
            for d in range(2)
        ]
        for k in range(2)
    ]
    to_y = [remote(ys_out, ys_in.at[i], sum_send, ys_s, y=t) for i, t in enumerate(at_y)]
    to_z = [remote(zs_out, zs_in.at[i], sum_send, zs_s, z=t) for i, t in enumerate(at_z)]
    to_far = [
        remote(far_out.at[i], far_in.at[i], sum_send, far_s, z=t, core=k)
        for i, t in ((0, z_down), (1, z_up))
        for k in range(2)
    ]
    to_mate = remote(tot, tot, sum_send, tot_s, core=0)

    def start(copies):
        for copy in copies:
            copy.start()

    def start_known(copies):
        for copy, to_late in copies:
            if to_late is None:
                copy.start()
            else:
                pl.when(jnp.logical_not(to_late))(copy.start)

    def start_late(copies):
        for copy, to_late in copies:
            if to_late is not None:
                pl.when(to_late)(copy.start)

    def wait_late():
        @pl.when(me != 0)
        def _():
            pl.semaphore_wait(late, 1)

    start(to_ones[1:])

    @pl.when(c == 0)
    def _():
        to_ones[0].start()

    scales.wait()
    start_known(to_scales)

    @pl.when((c == 0) | (2 * z < nz))
    def _():
        start_known(bulk)

    ii = lax.broadcasted_iota(jnp.int32, (rows, rows), 0)
    jj = lax.broadcasted_iota(jnp.int32, (rows, rows), 1)
    mat = lax.broadcasted_iota(jnp.int32, (slots, rows), 0)

    def column(values):
        row = jnp.sum(jnp.where(mat == x, values, 0.0), axis=0, keepdims=True)
        col = jnp.sum(jnp.where(ii == jj, row, 0.0), axis=1, keepdims=True)
        return jnp.broadcast_to(decay_rate * col, (rows, WIDTH))

    def columns():
        arrived(ms_in, ms_s, ms_send, core=other)
        for i in range(8):
            sc[i] = column(ms_in[i])

    @pl.when(c == 1)
    def _():
        total = xs_out[...]
        arrived(xs_in.at[pl.ds(0, 7)], xs_s, sum_send, core=0)
        for i in range(7):
            total = total + xs_in[i]
        wait_late()
        start_late(to_scales)

        @pl.when(2 * z < nz)
        def _():
            start_late(bulk)

        pl.semaphore_wait(barrier, len(at_y) + len(at_z) + (2 if far else 0))
        if y_near:
            ys_out[...] = total
            start(to_y)
            arrived(ys_in, ys_s, sum_send, y=at_y[0])
            for i in range(len(at_y)):
                total = total + ys_in[i]
        zs_out[...] = total
        start(to_z)

        ahead = behind = None
        if z_near:
            arrived(zs_in, zs_s, sum_send, z=at_z[0])
        for i, o in enumerate(z_near):
            total = total + zs_in[i]
            if o < 0:
                ahead = zs_in[i] if ahead is None else ahead + zs_in[i]
            elif o < REACH:
                behind = zs_in[i] if behind is None else behind + zs_in[i]
        if far:
            far_out[0] = ahead
            far_out[1] = behind
            start(to_far)
        tot[...] = total
        to_mate.start()

        @pl.when(2 * z >= nz)
        def _():
            start([copy for copy, _ in bulk])

        columns()

    @pl.when(c == 0)
    def _():
        wait_late()
        start_late(to_scales)

        start_late(bulk)
        columns()
        for k in range(2):
            arrived(hop.at[:, :, k], hop_s.at[k], bulk_send, x=xp, core=0)
            start(passed[k])
        arrived(tot, tot_s, sum_send, core=1)

    total = tot[...]
    if far:
        arrived(far_in, far_s, sum_send, z=z_up, core=1)
        total = total + far_in[0] + far_in[1]
    clip = lax.rsqrt(jnp.sum(total, axis=1, keepdims=True) / entries + epsilon)
    sent = []

    def send(*args, **where):
        copy = remote(*args, **where)
        copy.start()
        sent.append(copy)

    def gone(src, send_sem):
        remote(src, src, send_sem, raw_s, core=other).wait_send()

    def finish():
        for copy in sent:
            copy.wait_send()
        gone(ms_in.at[pl.ds(0, 7)], ms_send)
        gone(raw.at[:, pl.ds(0, 7)], bulk_send)

        @pl.when(c == 0)
        def _():
            gone(raw.at[:, pl.ds(0, 4)], fwd_send)
            gone(xs_in.at[pl.ds(0, 4)], sum_send)

        @pl.when(c == 1)
        def _():
            gone(counted.at[pl.ds(0, 4 + len(at_y) + len(at_z) + (4 if far else 0))], sum_send)

    arrived(raw, raw_s, bulk_send, core=other)

    tall = ff // 2
    for k in range(chunks):
        at = pl.ds(k * WIDTH, WIDTH)
        for i in range(8):
            xc[k, pl.ds(i * rows, rows)] = (
                raw[1, i, :, at].astype(F32) * sc[i] + clip * raw[0, i, :, at].astype(F32)
            ).astype(BF16)
        for r in range(2):
            part = dot_t(xc[k, pl.ds(r * tall, tall)], xc[k, pl.ds(r * tall, ff - r * tall)])
            to = gram.at[pl.ds(r * tall, tall), pl.ds(r * tall, ff - r * tall)]
            if k:
                part = to[...] + part
            to[...] = part
            if k == chunks - 1:
                blocks = [g_out.at[0], g_in.at[0]] if r == 0 else [ref.at[1, :, pl.ds(tall, tall)] for ref in (g_out, g_in)]
                blocks[0][...] = part.astype(BF16)
                send(blocks[0], blocks[1], g_s.at[0, r], g_s.at[1, r], x=x, core=other)
    norm = None
    diag = lax.broadcasted_iota(jnp.int32, (128, 128), 0) == lax.broadcasted_iota(jnp.int32, (128, 128), 1)
    for r in range(2):
        came_in = g_in.at[r, :, pl.ds(r * tall, ff - r * tall)]
        arrived(came_in, g_s.at[1, r], g_s.at[0, r], x=x, core=other)
        to = gram.at[pl.ds(r * tall, tall), pl.ds(r * tall, ff - r * tall)]
        whole = to[...] + came_in[...].astype(F32)
        to[...] = whole
        for b in range(tall // 128):
            square = whole[b * 128 : (b + 1) * 128, b * 128 : (b + 1) * 128]
            masked = jnp.where(diag, square, 0.0)
            norm = masked if norm is None else norm + masked
    norm = jnp.sum(jnp.sum(norm, axis=0, keepdims=True), axis=1, keepdims=True) + epsilon
    inverse = 1.0 / norm
    scale = (2.0 * half) ** 0.5 * lax.rsqrt(norm)

    upper = (gram[:tall] * inverse).astype(BF16)
    n_ref[:tall] = upper
    n_ref[tall:, :tall] = upper[:, tall:].T
    n_ref[tall:, tall:] = (gram[tall:, tall:] * inverse).astype(BF16)
    for r in range(2):
        at = pl.ds(r * tall, tall)
        eye = lax.broadcasted_iota(jnp.int32, (tall, ff), 0) + r * tall == lax.broadcasted_iota(jnp.int32, (tall, ff), 1)
        square = dot(n_ref[at], n_ref[...])
        p_ref[at] = (
            jnp.where(eye, coeff_linear, 0.0) + coeff_cubic * n_ref[at].astype(F32) + coeff_quintic * square
        ).astype(BF16)
    for r in range(2):
        at = pl.ds(r * tall, tall)
        halfway = dot(p_ref[at], n_ref[...]).astype(BF16)
        c_ref[at] = dot_t(halfway, p_ref[...]).astype(BF16)


    pair = 2 * rows

    def cols(k):
        return pl.ds(k * WIDTH, WIDTH)

    for i, chip in enumerate((x2, xp, xm, x)):
        at = pl.ds(pl.multiple_of(chip * pair, pair), pair)
        conj = c_ref[at]
        square = dot(conj, c_ref[...])
        quintic = (coeff_cubic * conj.astype(F32) + coeff_quintic * square).astype(BF16)
        product = dot(quintic, p_ref[...])
        final = (coeff_linear * p_ref[at].astype(F32) + product).astype(BF16)
        for k in range(chunks):
            u = (dot(final, xc[k]) * scale).astype(BF16)
            ubuf[i, 0, :, cols(k)] = u[:rows]
            ubuf[i, 1, :, cols(k)] = u[rows:]
        if i == 0:
            for d in range(2):
                remote(ubuf.at[0, d], uhop.at[d], o_send, o_hop.at[d], x=sides[d], core=c).start()
        elif i < 3:
            d = i - 1
            for h in range(2):
                remote(ubuf.at[i, h], out.at[x, :, mine], o_send, o_s, x=sides[d], core=h).start()
        else:
            send(ubuf.at[3, other], out.at[x, :, mine], o_mate, o_s, x=x, core=other)
            pltpu.make_async_copy(ubuf.at[3, c], out.at[x, :, mine], o_s).start()
    for d in range(2):
        arrived(uhop.at[d], o_hop.at[d], o_send, x=sides[d], core=c)
        remote(uhop.at[d], out.at[came[d], :, mine], o_send, o_s, x=sides[d], core=d).start()
    arrived(out, o_s, o_send, core=other)
    gone(ubuf, o_send)
    finish()


def per_device(mom_values, mom_scale, gradients):
    slots, rows, width = gradients.shape
    half, ff = width // 2, 8 * rows
    chunks = half // WIDTH
    sizes = (lax.axis_size("y"), lax.axis_size("z"))
    entries = float(gradients.size * 8 * sizes[0] * sizes[1])
    near = [max(len(far_first(n)), 1) for n in sizes]
    dma = pltpu.SemaphoreType.DMA

    def body(*refs):
        kernel(entries, sizes, *refs)

    return pl.pallas_call(
        body,
        out_shape=jax.ShapeDtypeStruct(mom_values.shape, BF16),
        in_specs=[pl.BlockSpec(memory_space=pltpu.HBM)] * 3,
        out_specs=pl.BlockSpec(memory_space=pltpu.VMEM),
        scratch_shapes=[
            pltpu.VMEM((slots, rows, width), BF16),
            pltpu.VMEM((1, 128), F32),
            pltpu.VMEM((8, 1, 128), F32),
            pltpu.VMEM((1, 128), F32),
            pltpu.VMEM((near[0], 1, 128), F32),
            pltpu.VMEM((1, 128), F32),
            pltpu.VMEM((near[1], 1, 128), F32),
            pltpu.VMEM((2, 1, 128), F32),
            pltpu.VMEM((2, 1, 128), F32),
            pltpu.VMEM((1, 128), F32),
            pltpu.VMEM((slots, rows), F32),
            pltpu.VMEM((8, slots, rows), F32),
            pltpu.VMEM((8, rows, WIDTH), F32),
            pltpu.VMEM((2, 2, 2, rows, half), BF16),
            pltpu.VMEM((2, 8, rows, half), BF16),
            pltpu.VMEM((chunks, ff, WIDTH), BF16),
            pltpu.VMEM((ff, ff), F32),
            pltpu.VMEM((2, ff // 2, ff), BF16),
            pltpu.VMEM((2, ff // 2, ff), BF16),
            pltpu.VMEM((ff, ff), BF16),
            pltpu.VMEM((ff, ff), BF16),
            pltpu.VMEM((ff, ff), BF16),
            pltpu.VMEM((4, 2, rows, half), BF16),
            pltpu.VMEM((2, rows, half), BF16),
            pltpu.VMEM((4 + sum(near) + 4, 1, 128), F32),
            pltpu.SemaphoreType.REGULAR,
            pltpu.SemaphoreType.REGULAR,
            dma((slots,)),
            dma,
            dma,
            dma,
            dma,
            dma,
            dma,
            dma,
            dma,
            dma,
            dma,
            dma((2,)),
            dma,
            dma,
            dma((2, 2)),
            dma,
            dma,
            dma((2,)),
            dma,
        ],
        compiler_params=pltpu.CompilerParams(
            collective_id=0, has_side_effects=True, vmem_limit_bytes=55_200_000
        ),
        name="muon",
    )(mom_values, pltpu.with_memory_space_constraint(mom_scale, pltpu.HBM), gradients)


def solution(mesh):
    finer = Mesh(mesh.devices.reshape(4, 2, 8, 16), AXES)
    return jax.shard_map(
        per_device,
        mesh=finer,
        in_specs=(P(EXPERT, ZERO, None), P(EXPERT, ZERO), P(EXPERT, ZERO, None)),
        out_specs=P(EXPERT, ZERO, None),
        check_vma=False,
    )
```

```python
import jax
import jax.numpy as jnp
from jax import lax
from jax.experimental import pallas as pl
from jax.experimental.pallas import tpu as pltpu
from jax.sharding import Mesh
from jax.sharding import PartitionSpec as P

AXES = ("x", "core", "y", "z")
ZERO = ("x", "core")
EXPERT = ("y", "z")

coeff_linear = 3.4445
coeff_cubic = -4.775
coeff_quintic = 2.0315
decay_rate = 0.95
epsilon = 1e-06

WIDTH = 256
REACH = 4
F32, BF16 = jnp.float32, jnp.bfloat16


def remote(src, dst, send_sem, recv_sem, **where):
    return pltpu.make_async_remote_copy(
        src_ref=src,
        dst_ref=dst,
        send_sem=send_sem,
        recv_sem=recv_sem,
        device_id=where,
        device_id_type=pl.DeviceIdType.MESH,
    )


def arrived(dst, recv_sem, send_sem, **where):
    remote(dst, dst, send_sem, recv_sem, **where).wait_recv()


def dot(a, b):
    return jnp.dot(a, b, preferred_element_type=F32)


def dot_t(a, b):
    return lax.dot_general(a, b, (((1,), (1,)), ((), ())), preferred_element_type=F32)


def far_first(n):
    if n > 2 * REACH:
        assert n == 4 * REACH
        return [o * s for o in range(REACH, 0, -1) for s in (1, -1)]
    return sorted(range(1, n), key=lambda o: -min(o, n - o))


def kernel(
    entries, sizes,
    mv, ms, gr, out,
    gbuf, xs_out, xs_in, ys_out, ys_in, zs_out, zs_in, far_out, far_in, tot,
    ms_own, ms_in, sc, hop, raw, xc, gram, g_out, g_in, n_ref, p_ref, c_ref, ubuf, uhop, counted,
    ready, late, loc_s, msl_s, sum_send, xs_s, ys_s, zs_s, far_s, tot_s, ms_send, ms_s, bulk_send, hop_s, fwd_send,
    raw_s, g_s, o_send, o_mate, o_hop, o_s,
):
    ny, nz = sizes
    slots, rows = gbuf.shape[:2]
    half = raw.shape[3]
    chunks = half // WIDTH
    ff = 8 * rows
    x, c, y, z = (lax.axis_index(a) for a in AXES)
    xp, xm, x2 = lax.rem(x + 1, 4), lax.rem(x + 3, 4), lax.rem(x + 2, 4)
    other = 1 - c
    me = 2 * x + c
    sides = (xp, xm)
    came = (xm, xp)
    y_near, z_near = far_first(ny), far_first(nz)
    at_y = [lax.rem(y + (o + ny), ny) for o in y_near]
    at_z = [lax.rem(z + (o + nz), nz) for o in z_near]
    z_up, z_down = lax.rem(z + REACH, nz), lax.rem(z + nz - REACH % nz, nz)
    far = nz > 2 * REACH
    at_x = [lax.rem(x + dx, 4) for dx in range(4)]
    from_x = [lax.rem(x + 4 - dx, 4) for dx in range(4)]
    group = [(dx, dc) for dx in (2, 1, 3, 0) for dc in (0, 1) if dx or dc]
    mine = pl.ds(pl.multiple_of(c * half, half), half)
    theirs = pl.ds(pl.multiple_of(other * half, half), half)
    mesh_ids = pl.DeviceIdType.MESH

    def member(dx, dc):
        return {"x": at_x[dx], "core": other if dc else c}

    barrier = pltpu.get_barrier_semaphore()
    for dx in (2, 1, 3, 0):

        @pl.when(((c == 1) | (dx != 0)) & (me != 0))
        def _():
            pl.semaphore_signal(barrier, inc=1, device_id={"x": at_x[dx], "core": 0}, device_id_type=mesh_ids)

    local = [pltpu.make_async_copy(gr.at[m], gbuf.at[m], loc_s.at[m]) for m in range(slots)]
    for copy in local:
        copy.start()
    if far:

        @pl.when(c == 0)
        def _():
            for t in (z_up, z_down):
                pl.semaphore_signal(barrier, inc=1, device_id={"z": t, "core": 1}, device_id_type=mesh_ids)

    @pl.when(c == 1)
    def _():
        for t in at_z:
            pl.semaphore_signal(barrier, inc=1, device_id={"z": t}, device_id_type=mesh_ids)
        for t in at_y:
            pl.semaphore_signal(barrier, inc=1, device_id={"y": t}, device_id_type=mesh_ids)

    scales = pltpu.make_async_copy(ms, ms_own, msl_s)
    scales.start()
    pltpu.make_async_copy(ms, ms_in.at[me], ms_s).start()
    for t, src in enumerate((gr, mv)):
        pltpu.make_async_copy(src.at[x, :, mine], raw.at[t, me], raw_s).start()

    @pl.when(c == 0)
    def _():
        pl.semaphore_wait(barrier, jnp.where(x == 0, 7, 6))

        @pl.when(x == 0)
        def _():
            for dx, dc in group:
                pl.semaphore_signal(late, inc=1, device_id=member(dx, dc), device_id_type=mesh_ids)

        @pl.when(x != 0)
        def _():
            pl.semaphore_signal(ready, inc=1, device_id={"core": 1}, device_id_type=mesh_ids)

        @pl.when(x == 1)
        def _():
            pl.semaphore_signal(ready, inc=1, device_id={"x": xm, "core": 1}, device_id_type=mesh_ids)

    acc = None
    for m in range(slots):
        local[m].wait()
        for h in range(2):
            g = gbuf[m, :, h * half : (h + 1) * half].astype(F32)
            part = jnp.sum((g * g).reshape(rows // 8, 8, half), axis=0)
            acc = part if acc is None else acc + part
    lanes = acc[:, :128]
    for i in range(1, half // 128):
        lanes = lanes + acc[:, i * 128 : (i + 1) * 128]
    xs_out[...] = jnp.sum(lanes, axis=0, keepdims=True)

    @pl.when(c == 1)
    def _():
        pl.semaphore_wait(ready, 1)

    to_ones = [remote(xs_out, xs_in.at[2 * ((dx + 3) % 4) + c], sum_send, xs_s, x=at_x[dx], core=1) for dx in range(4)]
    to_scales = [
        (
            remote(ms_own, ms_in.at[me], ms_send, ms_s, **member(dx, dc)),
            (at_x[dx] == 0) & ((c == 1) if dc else (c == 0)),
        )
        for dx, dc in group
    ]
    bulk = [
        (
            remote(
                src.at[x2, :, pl.ds(d * half, half)], hop.at[t, d, c],
                bulk_send, hop_s.at[c], x=sides[d], core=0,
            ),
            sides[d] == 0,
        )
        for t, src in enumerate((gr, mv))
        for d in range(2)
    ]
    for t, src in enumerate((gr, mv)):
        mate = remote(src.at[x, :, theirs], raw.at[t, me], bulk_send, raw_s, x=x, core=other)
        bulk.append((mate, me == 1))
        for d in range(2):
            for k in range(2):
                copy = remote(
                    src.at[sides[d], :, pl.ds(k * half, half)], raw.at[t, me],
                    bulk_send, raw_s, x=sides[d], core=k,
                )
                bulk.append((copy, sides[d] == 0 if k == 0 else None))
    origin = [[2 * came[d] + k for k in range(2)] for d in range(2)]
    passed = [
        [
            remote(
                hop.at[t, d, k], raw.at[t, origin[d][k]],
                fwd_send, raw_s, x=sides[d], core=d,
            )
            for t in range(2)
            for d in range(2)
        ]
        for k in range(2)
    ]
    to_y = [remote(ys_out, ys_in.at[i], sum_send, ys_s, y=t) for i, t in enumerate(at_y)]
    to_z = [remote(zs_out, zs_in.at[i], sum_send, zs_s, z=t) for i, t in enumerate(at_z)]
    to_far = [
        remote(far_out.at[i], far_in.at[i], sum_send, far_s, z=t, core=k)
        for i, t in ((0, z_down), (1, z_up))
        for k in range(2)
    ]
    to_mate = remote(tot, tot, sum_send, tot_s, core=0)

    def start(copies):
        for copy in copies:
            copy.start()

    def start_known(copies):
        for copy, to_late in copies:
            if to_late is None:
                copy.start()
            else:
                pl.when(jnp.logical_not(to_late))(copy.start)

    def start_late(copies):
        for copy, to_late in copies:
            if to_late is not None:
                pl.when(to_late)(copy.start)

    def wait_late():
        @pl.when(me != 0)
        def _():
            pl.semaphore_wait(late, 1)

    start(to_ones[1:])

    @pl.when(c == 0)
    def _():
        to_ones[0].start()

    scales.wait()
    start_known(to_scales)

    @pl.when((c == 0) | (2 * z < nz))
    def _():
        start_known(bulk)

    ii = lax.broadcasted_iota(jnp.int32, (rows, rows), 0)
    jj = lax.broadcasted_iota(jnp.int32, (rows, rows), 1)
    mat = lax.broadcasted_iota(jnp.int32, (slots, rows), 0)

    def column(values):
        row = jnp.sum(jnp.where(mat == x, values, 0.0), axis=0, keepdims=True)
        col = jnp.sum(jnp.where(ii == jj, row, 0.0), axis=1, keepdims=True)
        return jnp.broadcast_to(decay_rate * col, (rows, WIDTH))

    def columns():
        arrived(ms_in, ms_s, ms_send, core=other)
        for i in range(8):
            sc[i] = column(ms_in[i])

    @pl.when(c == 1)
    def _():
        total = xs_out[...]
        arrived(xs_in.at[pl.ds(0, 7)], xs_s, sum_send, core=0)
        for i in range(7):
            total = total + xs_in[i]
        wait_late()
        start_late(to_scales)

        @pl.when(2 * z < nz)
        def _():
            start_late(bulk)

        pl.semaphore_wait(barrier, len(at_y) + len(at_z) + (2 if far else 0))
        if y_near:
            ys_out[...] = total
            start(to_y)
            arrived(ys_in, ys_s, sum_send, y=at_y[0])
            for i in range(len(at_y)):
                total = total + ys_in[i]
        zs_out[...] = total
        start(to_z)

        ahead = behind = None
        if z_near:
            arrived(zs_in, zs_s, sum_send, z=at_z[0])
        for i, o in enumerate(z_near):
            total = total + zs_in[i]
            if o < 0:
                ahead = zs_in[i] if ahead is None else ahead + zs_in[i]
            elif o < REACH:
                behind = zs_in[i] if behind is None else behind + zs_in[i]
        if far:
            far_out[0] = ahead
            far_out[1] = behind
            start(to_far)
        tot[...] = total
        to_mate.start()

        @pl.when(2 * z >= nz)
        def _():
            start([copy for copy, _ in bulk])

        columns()

    @pl.when(c == 0)
    def _():
        wait_late()
        start_late(to_scales)

        start_late(bulk)
        columns()
        for k in range(2):
            arrived(hop.at[:, :, k], hop_s.at[k], bulk_send, x=xp, core=0)
            start(passed[k])
        arrived(tot, tot_s, sum_send, core=1)

    total = tot[...]
    if far:
        arrived(far_in, far_s, sum_send, z=z_up, core=1)
        total = total + far_in[0] + far_in[1]
    clip = lax.rsqrt(jnp.sum(total, axis=1, keepdims=True) / entries + epsilon)
    sent = []

    def send(*args, **where):
        copy = remote(*args, **where)
        copy.start()
        sent.append(copy)

    def gone(src, send_sem):
        remote(src, src, send_sem, raw_s, core=other).wait_send()

    def finish():
        for copy in sent:
            copy.wait_send()
        gone(ms_in.at[pl.ds(0, 7)], ms_send)
        gone(raw.at[:, pl.ds(0, 7)], bulk_send)

        @pl.when(c == 0)
        def _():
            gone(raw.at[:, pl.ds(0, 4)], fwd_send)
            gone(xs_in.at[pl.ds(0, 4)], sum_send)

        @pl.when(c == 1)
        def _():
            gone(counted.at[pl.ds(0, 4 + len(at_y) + len(at_z) + (4 if far else 0))], sum_send)

    arrived(raw, raw_s, bulk_send, core=other)

    tall = ff // 2
    for k in range(chunks):
        at = pl.ds(k * WIDTH, WIDTH)
        for i in range(8):
            xc[k, pl.ds(i * rows, rows)] = (
                raw[1, i, :, at].astype(F32) * sc[i] + clip * raw[0, i, :, at].astype(F32)
            ).astype(BF16)
        for r in range(2):
            part = dot_t(xc[k, pl.ds(r * tall, tall)], xc[k, pl.ds(r * tall, ff - r * tall)])
            to = gram.at[pl.ds(r * tall, tall), pl.ds(r * tall, ff - r * tall)]
            if k:
                part = to[...] + part
            to[...] = part
            if k == chunks - 1:
                blocks = [g_out.at[0], g_in.at[0]] if r == 0 else [ref.at[1, :, pl.ds(tall, tall)] for ref in (g_out, g_in)]
                blocks[0][...] = part.astype(BF16)
                send(blocks[0], blocks[1], g_s.at[0, r], g_s.at[1, r], x=x, core=other)
    norm = None
    diag = lax.broadcasted_iota(jnp.int32, (128, 128), 0) == lax.broadcasted_iota(jnp.int32, (128, 128), 1)
    for r in range(2):
        came_in = g_in.at[r, :, pl.ds(r * tall, ff - r * tall)]
        arrived(came_in, g_s.at[1, r], g_s.at[0, r], x=x, core=other)
        to = gram.at[pl.ds(r * tall, tall), pl.ds(r * tall, ff - r * tall)]
        whole = to[...] + came_in[...].astype(F32)
        to[...] = whole
        for b in range(tall // 128):
            square = whole[b * 128 : (b + 1) * 128, b * 128 : (b + 1) * 128]
            masked = jnp.where(diag, square, 0.0)
            norm = masked if norm is None else norm + masked
    norm = jnp.sum(jnp.sum(norm, axis=0, keepdims=True), axis=1, keepdims=True) + epsilon
    inverse = 1.0 / norm
    scale = (2.0 * half) ** 0.5 * lax.rsqrt(norm)

    upper = (gram[:tall] * inverse).astype(BF16)
    n_ref[:tall] = upper
    n_ref[tall:, :tall] = upper[:, tall:].T
    n_ref[tall:, tall:] = (gram[tall:, tall:] * inverse).astype(BF16)
    eye = lax.broadcasted_iota(jnp.int32, (ff, ff), 0) == lax.broadcasted_iota(jnp.int32, (ff, ff), 1)
    square = dot(n_ref[...], n_ref[...])
    p_ref[...] = (
        jnp.where(eye, coeff_linear, 0.0) + coeff_cubic * n_ref[...].astype(F32) + coeff_quintic * square
    ).astype(BF16)
    halfway = dot(p_ref[...], n_ref[...]).astype(BF16)
    c_ref[...] = dot_t(halfway, p_ref[...]).astype(BF16)

    pair = 2 * rows

    def cols(k):
        return pl.ds(k * WIDTH, WIDTH)

    for i, chip in enumerate((x2, xp, xm, x)):
        at = pl.ds(pl.multiple_of(chip * pair, pair), pair)
        conj = c_ref[at]
        square = dot(conj, c_ref[...])
        quintic = (coeff_cubic * conj.astype(F32) + coeff_quintic * square).astype(BF16)
        product = dot(quintic, p_ref[...])
        final = (coeff_linear * p_ref[at].astype(F32) + product).astype(BF16)
        for k in range(chunks):
            u = (dot(final, xc[k]) * scale).astype(BF16)
            ubuf[i, 0, :, cols(k)] = u[:rows]
            ubuf[i, 1, :, cols(k)] = u[rows:]
        if i == 0:
            for d in range(2):
                remote(ubuf.at[0, d], uhop.at[d], o_send, o_hop.at[d], x=sides[d], core=c).start()
        elif i < 3:
            d = i - 1
            for h in range(2):
                remote(ubuf.at[i, h], out.at[x, :, mine], o_send, o_s, x=sides[d], core=h).start()
        else:
            send(ubuf.at[3, other], out.at[x, :, mine], o_mate, o_s, x=x, core=other)
            pltpu.make_async_copy(ubuf.at[3, c], out.at[x, :, mine], o_s).start()
    for d in range(2):
        arrived(uhop.at[d], o_hop.at[d], o_send, x=sides[d], core=c)
        remote(uhop.at[d], out.at[came[d], :, mine], o_send, o_s, x=sides[d], core=d).start()
    arrived(out, o_s, o_send, core=other)
    gone(ubuf, o_send)
    finish()


def per_device(mom_values, mom_scale, gradients):
    slots, rows, width = gradients.shape
    half, ff = width // 2, 8 * rows
    chunks = half // WIDTH
    sizes = (lax.axis_size("y"), lax.axis_size("z"))
    entries = float(gradients.size * 8 * sizes[0] * sizes[1])
    near = [max(len(far_first(n)), 1) for n in sizes]
    dma = pltpu.SemaphoreType.DMA

    def body(*refs):
        kernel(entries, sizes, *refs)

    return pl.pallas_call(
        body,
        out_shape=jax.ShapeDtypeStruct(mom_values.shape, BF16),
        in_specs=[pl.BlockSpec(memory_space=pltpu.HBM)] * 3,
        out_specs=pl.BlockSpec(memory_space=pltpu.VMEM),
        scratch_shapes=[
            pltpu.VMEM((slots, rows, width), BF16),
            pltpu.VMEM((1, 128), F32),
            pltpu.VMEM((8, 1, 128), F32),
            pltpu.VMEM((1, 128), F32),
            pltpu.VMEM((near[0], 1, 128), F32),
            pltpu.VMEM((1, 128), F32),
            pltpu.VMEM((near[1], 1, 128), F32),
            pltpu.VMEM((2, 1, 128), F32),
            pltpu.VMEM((2, 1, 128), F32),
            pltpu.VMEM((1, 128), F32),
            pltpu.VMEM((slots, rows), F32),
            pltpu.VMEM((8, slots, rows), F32),
            pltpu.VMEM((8, rows, WIDTH), F32),
            pltpu.VMEM((2, 2, 2, rows, half), BF16),
            pltpu.VMEM((2, 8, rows, half), BF16),
            pltpu.VMEM((chunks, ff, WIDTH), BF16),
            pltpu.VMEM((ff, ff), F32),
            pltpu.VMEM((2, ff // 2, ff), BF16),
            pltpu.VMEM((2, ff // 2, ff), BF16),
            pltpu.VMEM((ff, ff), BF16),
            pltpu.VMEM((ff, ff), BF16),
            pltpu.VMEM((ff, ff), BF16),
            pltpu.VMEM((4, 2, rows, half), BF16),
            pltpu.VMEM((2, rows, half), BF16),
            pltpu.VMEM((4 + sum(near) + 4, 1, 128), F32),
            pltpu.SemaphoreType.REGULAR,
            pltpu.SemaphoreType.REGULAR,
            dma((slots,)),
            dma,
            dma,
            dma,
            dma,
            dma,
            dma,
            dma,
            dma,
            dma,
            dma,
            dma((2,)),
            dma,
            dma,
            dma((2, 2)),
            dma,
            dma,
            dma((2,)),
            dma,
        ],
        compiler_params=pltpu.CompilerParams(
            collective_id=0, has_side_effects=True, vmem_limit_bytes=55_200_000
        ),
        name="muon",
    )(mom_values, pltpu.with_memory_space_constraint(mom_scale, pltpu.HBM), gradients)


def solution(mesh):
    finer = Mesh(mesh.devices.reshape(4, 2, 8, 16), AXES)
    return jax.shard_map(
        per_device,
        mesh=finer,
        in_specs=(P(EXPERT, ZERO, None), P(EXPERT, ZERO), P(EXPERT, ZERO, None)),
        out_specs=P(EXPERT, ZERO, None),
        check_vma=False,
    )
```
